32 devices in a mesh: aa: 4 (over z), ba: 8 (over y, x, core).
Axes of the slice: x: 2, y: 2, z: 4, core: 2. Of those that a mesh axis runs over, the one named last changes fastest.
Arguments:
- feats: bfloat16 [4, 32, 128, 256], P('aa', 'ba'), may hold values from -6 to 6
- conv_one: bfloat16 [3, 3, 3, 256, 256], replicated, may hold values from -0.078125 to 0.078125
- bias_one: float32 [256], replicated, may hold values from -3 to 3
- conv_two: bfloat16 [3, 3, 3, 256, 256], replicated, may hold values from -0.078125 to 0.078125
- bias_two: float32 [256], replicated, may hold values from -3 to 3
- patch_weight: bfloat16 [2, 2, 256, 128], replicated, may hold values from -0.1875 to 0.1875
- patch_bias: float32 [128], replicated, may hold values from -3 to 3
- embed_weight: bfloat16 [128, 2048], replicated, may hold values from -0.5 to 0.5
- embed_bias: float32 [2048], replicated, may hold values from -6 to 6
- norm_gain: float32 [2048], replicated, may hold values from 0.1 to 1.9
- w_query: bfloat16 [2048, 2048], P(None, 'ba'), may hold values from -2 to 2
- w_key: bfloat16 [2048, 2048], P(None, 'ba'), may hold values from -2 to 2
- w_value: bfloat16 [2048, 2048], P(None, 'ba'), may hold values from -0.125 to 0.125
- w_velocity: bfloat16 [2048, 128], P('ba'), may hold values from -0.5 to 0.5
Outputs:
- velocity: float32 [4096, 128], P(('aa', 'ba'))
The draws below stay inside these ranges and needn't reach their ends.
All inputs are finite; a program needn't handle non-finite values.
Results may differ from the reference program's by a relative error of at most 0.035.
Values may be sent and summed in bfloat16 or wider, within the bound.
A program may use at most 128 MiB of HBM per device.

```python
import math
import jax
import jax.numpy as jnp
from jax import lax

C = 256
LAT = 128
D = 2048
HEADS = 32
HEAD_DIM = 64
FT = 1
SH = 4
W = 128
TOKENS = 4096
FRAMES = 4
ROWS = 32
N_AA = 4
N_BA = 8


def shared_query(key):
    return jax.random.normal(jax.random.fold_in(key, 11), (D, D), jnp.float32) * D ** (-0.5)


def draw_w_query(key, part):
    return jnp.clip(shared_query(key), -2.0, 2.0).astype(jnp.bfloat16)


def draw_w_key(key, part):
    noise = jax.random.normal(jax.random.fold_in(key, 23), (D, D), jnp.float32) * (4.0 * D ** (-0.5))
    return jnp.clip(noise, -2.0, 2.0).astype(jnp.bfloat16)


def levels(own_key, dims, cuts, smallest, high):
    def one(axis_at, blocks):
        draws = jax.random.uniform(jax.random.fold_in(jax.random.fold_in(own_key, 6), axis_at), (blocks,), jnp.float32, smallest / len(cuts), high / len(cuts))
        return jnp.repeat(jnp.exp(draws), dims[axis_at] // blocks).reshape((-1,) + (1,) * (len(dims) - axis_at - 1))

    gain = one(*cuts[0])
    for cut in cuts[1:]:
        gain = gain * one(*cut)
    return gain


def scatter_about(own_key, extent, deviation, reach, cuts=(), dtype=jnp.bfloat16):
    values = deviation * jax.random.normal(own_key, extent, jnp.float32)
    if cuts:
        values = values * levels(own_key, extent, cuts, -0.22, 0.18)
    return jnp.clip(values, -reach, reach).astype(dtype)


def setup_inputs(seed: int = 0) -> dict:
    key_list = jax.random.split(jax.random.key(seed), 15)
    return {
        "feats": scatter_about(key_list[0], (FRAMES, ROWS, W, C), 1.0, 6.0, ((0, 4), (1, 8))),
        "conv_one": scatter_about(key_list[1], (3, 3, 3, C, C), (27 * C) ** -0.5, 0.078125),
        "bias_one": scatter_about(key_list[2], (C,), 0.5, 3.0, (), jnp.float32),
        "conv_two": scatter_about(key_list[3], (3, 3, 3, C, C), (27 * C) ** -0.5, 0.078125),
        "bias_two": scatter_about(key_list[4], (C,), 0.5, 3.0, (), jnp.float32),
        "patch_weight": scatter_about(key_list[5], (2, 2, C, LAT), (4 * C) ** -0.5, 0.1875),
        "patch_bias": scatter_about(key_list[6], (LAT,), 0.5, 3.0, (), jnp.float32),
        "embed_weight": scatter_about(key_list[7], (LAT, D), LAT ** -0.5, 0.5),
        "embed_bias": scatter_about(key_list[8], (D,), 1.0, 6.0, (), jnp.float32),
        "norm_gain": jnp.clip(1.0 + 0.18 * jax.random.normal(key_list[9], (D,), jnp.float32), 0.1, 1.9),
        "w_query": draw_w_query(jax.random.fold_in(key_list[14], 71), 0),
        "w_key": draw_w_key(jax.random.fold_in(key_list[14], 71), 0),
        "w_value": scatter_about(key_list[12], (D, D), D ** -0.5, 0.125, ((1, 8),)),
        "w_velocity": scatter_about(key_list[13], (D, LAT), (D // 16) ** -0.5, 0.5, ((0, 8),)),
    }


def convolve(field, kernel, bias):
    frames, rows, width, chans = field.shape
    padded = jnp.pad(field, ((1, 1), (1, 1), (1, 1), (0, 0)))
    total = jnp.zeros((frames * rows * width, kernel.shape[-1]), jnp.float32)
    for shift_t in range(3):
        for shift_r in range(3):
            window = padded[shift_t:shift_t + frames, shift_r:shift_r + rows]
            stacked = jnp.concatenate([window[:, :, shift_w:shift_w + width] for shift_w in range(3)], axis=-1)
            total = total + jnp.dot(stacked.reshape(-1, 3 * chans), kernel[shift_t, shift_r].reshape(3 * chans, -1), preferred_element_type=jnp.float32)
    return (total + bias).reshape(frames, rows, width, -1)

def patchify(field, weight, bias):
    frames, rows, width, chans = field.shape
    blocks = field.reshape(frames, rows // 2, 2, width // 2, 2, chans).transpose(0, 1, 3, 2, 4, 5).reshape(-1, 4 * chans)
    return (jnp.dot(blocks, weight.reshape(4 * chans, -1), preferred_element_type=jnp.float32) + bias).astype(jnp.bfloat16)

def normalize(latent_rows, embed_weight, embed_bias, norm_gain):
    hidden = jnp.dot(latent_rows, embed_weight, preferred_element_type=jnp.float32) + embed_bias
    center = hidden - hidden.mean(-1, keepdims=True)
    spread = (center * center).mean(-1, keepdims=True)
    return (center * lax.rsqrt(spread + 1e-05) * norm_gain).astype(jnp.bfloat16)

def head_attention(trio):
    query_head, key_head, value_head = trio
    scale = HEAD_DIM ** (-0.5)
    count = math.gcd(TOKENS, 1024)

    def one_block(query_block):
        scores = jnp.dot(query_block, key_head.T, preferred_element_type=jnp.float32) * scale
        probs = jnp.exp(scores - scores.max(-1, keepdims=True))
        denom = probs.sum(-1, keepdims=True)
        return (jnp.dot(probs.astype(jnp.bfloat16), value_head, preferred_element_type=jnp.float32) / denom).astype(jnp.bfloat16)
    return lax.map(one_block, query_head.reshape(-1, count, HEAD_DIM)).reshape(TOKENS, HEAD_DIM)

def reference(feats, conv_one, bias_one, conv_two, bias_two, patch_weight, patch_bias, embed_weight, embed_bias, norm_gain, w_query, w_key, w_value, w_velocity):
    first = jax.nn.gelu(convolve(feats, conv_one, bias_one), approximate=False).astype(jnp.bfloat16)
    second = (first.astype(jnp.float32) + jax.nn.gelu(convolve(first, conv_two, bias_two), approximate=False)).astype(jnp.bfloat16)
    patches = patchify(second, patch_weight, patch_bias)
    latents = patches.reshape(N_AA, FT, N_BA, SH // 2, W // 2, LAT).transpose(0, 2, 1, 3, 4, 5).reshape(TOKENS, LAT)
    normed = normalize(latents, embed_weight, embed_bias, norm_gain)
    queries = jnp.dot(normed, w_query, preferred_element_type=jnp.float32).astype(jnp.bfloat16)
    keys = jnp.dot(normed, w_key, preferred_element_type=jnp.float32).astype(jnp.bfloat16)
    values = jnp.dot(normed, w_value, preferred_element_type=jnp.float32).astype(jnp.bfloat16)

    def split_heads(matrix):
        return matrix.reshape(TOKENS, HEADS, HEAD_DIM).transpose(1, 0, 2)
    attended = lax.map(head_attention, (split_heads(queries), split_heads(keys), split_heads(values)))
    attended = attended.transpose(1, 0, 2).reshape(TOKENS, D)
    return jnp.dot(attended, w_velocity, preferred_element_type=jnp.float32)
```

```python
import functools
import math

import jax
import jax.numpy as jnp
from jax import lax
from jax.experimental import pallas as pl
from jax.experimental.pallas import tpu as pltpu
from jax.sharding import PartitionSpec as P

HEAD_DIM = 64
SLOT = 128
MESH = pl.DeviceIdType.MESH
GROUP = 2
LOOK = 2
STACK = HEAD_DIM + 16
F32 = jnp.float32
BF16 = jnp.bfloat16
VMEM_BYTES = 67043328


def dot(left, right):
    return jnp.dot(left, right, preferred_element_type=F32)


def two_parts(value):
    high = value.astype(BF16)
    return high, (value - high.astype(F32)).astype(BF16)


def gelu(value):
    return 0.5 * value * (1.0 + lax.erf(value * (0.5**0.5)))


def whole_kernel(
    n_aa, n_ba, span, chunk,
    feats, conv_one, bias_one, conv_two, bias_two, patch_weight, patch_bias,
    embed_weight, embed_bias, norm_gain, w_query, w_key, w_value, w_velocity,
    out,
    field, taps, w_joined, outgoing, incoming, acc, pair, gathered, split, offsets, turned, lift,
    gram_split, gram, queries, keys, values, attended, shares, arrived,
    load_sem, aa_side_send, aa_side_recv, ba_side_send, ba_side_recv,
    token_recv, aa_send, ba_send, core_send, share_send, share_recv,
):
    aa, ba = lax.axis_index("aa"), lax.axis_index("ba")
    _, rows, width, chans = feats.shape
    partner = ba + 1 - 2 * (ba % 2)
    half = n_ba // 2
    width_q = w_query.shape[1]
    heads = width_q // HEAD_DIM
    tokens = rows * width // 4
    lat = patch_bias.shape[1]

    def load(source, target, at):
        return pltpu.make_async_copy(source, target, load_sem.at[at])

    loads = [
        load(feats.at[0], field.at[0, 1, pl.ds(1, rows)], 0),
        load(w_query, w_joined.at[0], 1),
        load(w_key, w_joined.at[1], 2),
        load(w_value, w_joined.at[2], 3),
    ]
    kernels = [
        [load(source.at[at], taps.at[which, :, :, pl.ds(column * chans, chans)], 4 + 3 * which + at)
         for at, column in enumerate((0, 2, 1))]
        for which, source in enumerate((conv_one, conv_two))
    ]
    loads[0].start()
    for at in (0, 2, 1):
        kernels[0][at].start()
    for one in loads[1:]:
        one.start()
    for at in (0, 2, 1):
        kernels[1][at].start()

    def aa_there(side):
        return aa > 0 if side == -1 else aa < n_aa - 1

    def ba_there(side):
        return ba > 0 if side == -1 else ba < n_ba - 1

    barrier = pltpu.get_barrier_semaphore()
    for step in range(1, n_aa):
        pl.semaphore_signal(
            barrier, inc=1, device_id=((aa + step) % n_aa, ba), device_id_type=MESH
        )
    for step in range(1, n_ba):
        pl.semaphore_signal(
            barrier, inc=1, device_id=(aa, (ba + step) % n_ba), device_id_type=MESH
        )

    edges, middle, both = 0, 1, 2
    parts = (slice(0, 2), slice(2, rows))

    def along_time(which, side, part):
        at = (which, (side + 1) // 2, part)
        here = (which, (side + 1) // 2, parts[part])
        return pltpu.make_async_remote_copy(
            src_ref=outgoing.at[here], dst_ref=incoming.at[here],
            send_sem=aa_side_send.at[at], recv_sem=aa_side_recv.at[at],
            device_id=(aa + side, ba), device_id_type=MESH,
        )

    def along_rows(which, side):
        source, target = (rows, 0) if side == 1 else (1, rows + 1)
        at = (which, (side + 1) // 2)
        return pltpu.make_async_remote_copy(
            src_ref=field.at[which, 1, source], dst_ref=field.at[which, 1, target],
            send_sem=ba_side_send.at[at], recv_sem=ba_side_recv.at[at],
            device_id=(aa, ba + side), device_id_type=MESH,
        )

    def send_rows(which):
        for side in (-1, 1):
            pl.when(ba_there(side))(along_rows(which, side).start)

    def take_rows(which):
        for side in (-1, 1):
            pl.when(ba_there(-side))(along_rows(which, side).wait_recv)
        shift(which, 0, 1)
        shift(which, rows + 1, 1)

    def take_time(which, part):
        for side in (-1, 1):
            pl.when(aa_there(-side))(along_time(which, side, part).wait_recv)

    def sent(which):
        for side in (-1, 1):
            pl.when(ba_there(side))(along_rows(which, side).wait_send)
            for part in (edges, middle):
                pl.when(aa_there(side))(along_time(which, side, part).wait_send)

    def blank():
        line = jnp.zeros((width, chans), BF16)
        for which in range(2):
            for side, row in ((-1, 0), (1, rows + 1)):
                @pl.when(jnp.logical_not(ba_there(side)))
                def _():
                    field[which, 1, row] = line

                @pl.when(jnp.logical_not(aa_there(side)))
                def _():
                    for at in range(rows):
                        incoming[which, (1 - side) // 2, at] = line

    def shift(which, row, count):
        here = pl.ds(row, count)
        held = field[which, 1, here].reshape(count * width, chans).astype(F32)
        place = lax.broadcasted_iota(jnp.int32, held.shape, 0) % width
        before = jnp.where(place == 0, 0.0, pltpu.roll(held, 1, 0))
        after = jnp.where(place == width - 1, 0.0, pltpu.roll(held, count * width - 1, 0))
        field[which, 0, here] = before.astype(BF16).reshape(count, width, chans)
        field[which, 2, here] = after.astype(BF16).reshape(count, width, chans)

    def stack(which, part):
        def window(shift_r, shift_w):
            if part == middle:
                held = field[which, shift_w, pl.ds(1 + shift_r, rows - 2)]
                return held.reshape((rows - 2) * width, chans)
            if part == both:
                return field[which, shift_w, pl.ds(shift_r, rows)].reshape(rows * width, chans)
            return jnp.concatenate(
                [field[which, shift_w, shift_r], field[which, shift_w, rows - 1 + shift_r]], axis=0
            )

        return jnp.concatenate(
            [window(shift_r, shift_w) for shift_r in range(3) for shift_w in range(3)], axis=1
        )

    def send_time(which, part):
        made = dot(
            stack(which, part), taps[which, :, :, : 2 * chans].reshape(9 * chans, 2 * chans)
        ).astype(BF16)
        for side, column in ((-1, chans), (1, 0)):
            outgoing[which, (side + 1) // 2, parts[part]] = made[
                :, column : column + chans
            ].reshape(-1, width, chans)
            pl.when(aa_there(side))(along_time(which, side, part).start)

    def keep(which):
        acc[...] = dot(
            stack(which, both), taps[which, :, :, 2 * chans :].reshape(9 * chans, chans)
        ).reshape(rows, width, chans)

    def activate(which, part, bias):
        here = parts[part]
        kept = acc[1 : rows - 1] if part == middle else jnp.concatenate(
            [acc[:1], acc[rows - 1 :]], axis=0
        )
        total = kept + incoming[which, 0, here].astype(F32)
        total += incoming[which, 1, here].astype(F32)
        return gelu(total.reshape(-1, chans) + bias)

    blank()
    loads[0].wait()
    shift(0, 1, rows)
    pl.semaphore_wait(barrier, n_aa - 1 + n_ba - 1)
    send_rows(0)
    kernels[0][0].wait()
    kernels[0][2].wait()
    send_time(0, middle)
    take_rows(0)
    send_time(0, edges)

    def merge_weights():
        embed = embed_weight[...].astype(F32)
        centred = jnp.concatenate(
            [
                embed - embed.mean(-1, keepdims=True),
                jnp.broadcast_to(
                    embed_bias[...] - embed_bias[...].mean(-1, keepdims=True),
                    (8, embed.shape[1]),
                ),
            ],
            axis=0,
        )
        gram[...] = lax.dot_general(
            centred, centred, (((1,), (1,)), ((), ())),
            precision=lax.Precision.HIGHEST, preferred_element_type=F32,
        ) * (1.0 / embed.shape[1])
        high, low = two_parts(gram[:lat, :lat])
        gram_split[:lat] = high
        gram_split[lat:] = low
        turned[width_q : width_q + lat, :lat] = high
        turned[width_q : width_q + lat, lat:] = low
        across = lax.broadcasted_iota(jnp.int32, (lat, 2 * lat), 1)
        down = lax.broadcasted_iota(jnp.int32, (lat, 2 * lat), 0)
        turned[width_q + lat :] = (across == down).astype(BF16)
        gained = jnp.concatenate(two_parts(centred * norm_gain[...]), axis=0)
        for which in range(3):
            loads[1 + which].wait()
            product = dot(gained, w_joined[which])
            product = product[: lat + 8] + product[lat + 8 :]
            if which == 2:
                high, low = two_parts(product[:lat].T)
                turned[:width_q, :lat] = high
                turned[:width_q, lat:] = low
                lift[...] = product[lat:].T
                continue
            if which == 0:
                product = product * (HEAD_DIM**-0.5 * math.log2(math.e))
            blanks = jnp.zeros((product.shape[0], SLOT - HEAD_DIM), F32)
            for head in range(heads):
                piece = jnp.concatenate(
                    [product[:, head * HEAD_DIM : (head + 1) * HEAD_DIM], blanks], axis=1
                )
                slot = slice(head * SLOT, (head + 1) * SLOT)
                high, low = two_parts(piece[:lat])
                split[which, :lat, slot] = high
                split[which, lat:, slot] = low
                offsets[which, :, slot] = piece[lat:]

    kernels[0][1].wait()
    keep(0)
    merge_weights()
    take_time(0, middle)
    take_time(0, edges)
    first = activate(0, edges, bias_one[...]).astype(BF16)
    field[1, 1, 1] = first[:width]
    field[1, 1, rows] = first[width:]
    send_rows(1)
    first = activate(0, middle, bias_one[...]).astype(BF16)
    field[1, 1, 2:rows] = first.reshape(-1, width, chans)
    shift(1, 1, rows)
    for at in (0, 2, 1):
        kernels[1][at].wait()
    send_time(1, middle)
    take_rows(1)
    send_time(1, edges)
    keep(1)

    def finish(part):
        here = field[1, 1, 2:rows] if part == middle else jnp.concatenate(
            [field[1, 1, 1], field[1, 1, rows]], axis=0
        )
        own = here.reshape(-1, chans).astype(F32)
        return (own + activate(1, part, bias_two[...])).astype(BF16)

    take_time(1, middle)
    inner = finish(middle)
    take_time(1, edges)
    outer = finish(edges)
    lines = [outer[:width]]
    lines += [inner[at * width : (at + 1) * width] for at in range(rows - 2)]
    lines += [outer[width:]]

    line = width // 2
    for block in range(rows // 2):
        for col in range(2):
            pair[col] = dot(lines[2 * block], patch_weight[0, col]) + dot(
                lines[2 * block + 1], patch_weight[1, col]
            )
        patches = (
            pair[0, pl.ds(0, line, stride=2), :] + pair[1, pl.ds(1, line, stride=2), :]
            + patch_bias[...]
        ).astype(BF16)
        gathered[aa, ba, pl.ds(block * line, line), :] = patches

    turn = jnp.where(aa < n_aa // 2, 1, n_aa - 1)
    values[:, HEAD_DIM:] = jnp.ones((heads, values.shape[1] - HEAD_DIM, values.shape[2]), BF16)

    def frame_of(step):
        return (aa + turn * step) % n_aa

    def piece(frame, block, send_sem, to_aa, to_ba):
        here = gathered.at[frame, block]
        return pltpu.make_async_remote_copy(
            src_ref=here, dst_ref=here, send_sem=send_sem, recv_sem=token_recv.at[frame, block],
            device_id=(to_aa, to_ba), device_id_type=MESH,
        )

    def along_aa(step):
        return piece(aa, ba, aa_send.at[step], (aa + n_aa - turn * step + n_aa * n_aa) % n_aa, ba)

    def along_ba(step, hop):
        return piece(frame_of(step), ba, ba_send.at[step, hop], aa, (ba + 2 * hop) % n_ba)

    def to_partner(step, hop):
        block = (ba + n_ba - 2 * hop) % n_ba
        return piece(frame_of(step), block, core_send.at[step, hop], aa, partner)

    def landed(frame, block):
        piece(frame, block, aa_send.at[0], aa, partner).wait_recv()

    slope = 2.0 * gram[lat : lat + 1, :lat]
    slope_down = 2.0 * gram[:lat, lat : lat + 1]
    floor = gram[lat : lat + 1, lat : lat + 1]

    def take_pair(step, hop, with_queries):
        frame = frame_of(step)
        block = ((ba + n_ba - 2 * hop) % n_ba) // 2
        latents = gathered[frame, pl.ds(2 * block, 2)].reshape(2 * tokens, lat)
        twice = jnp.concatenate([latents, latents], axis=1)
        bent = dot(twice, gram_split[...]) + slope
        power = (bent * latents.astype(F32)).sum(-1, keepdims=True) + floor
        scale = lax.rsqrt(jnp.maximum(power, 0.0) + 1e-05)
        at = pl.multiple_of((frame * half + block) * 2 * tokens, 2 * tokens)
        projected = ((dot(twice, split[1]) + offsets[1, :1]) * scale).astype(BF16)
        for head in range(heads):
            keys[head, pl.ds(at, 2 * tokens)] = projected[:, head * SLOT : (head + 1) * SLOT]
        down = lax.dot_general(
            turned[...], twice, (((1,), (1,)), ((), ())), preferred_element_type=F32
        )
        bent = (down[width_q : width_q + lat] + slope_down) * down[width_q + lat :]
        power = bent.sum(0, keepdims=True) + floor
        scale_down = lax.rsqrt(jnp.maximum(power, 0.0) + 1e-05)
        flipped = ((down[:width_q] + lift[:, :1]) * scale_down).astype(BF16)
        for head in range(heads):
            values[head, :HEAD_DIM, pl.ds(at, 2 * tokens)] = flipped[
                head * HEAD_DIM : (head + 1) * HEAD_DIM
            ]
        if with_queries:
            asked = ((dot(twice, split[0]) + offsets[0, :1]) * scale).astype(BF16)
            there = pl.ds(pl.multiple_of(block * 2 * tokens, 2 * tokens), 2 * tokens)
            for head in range(heads):
                queries[head, there] = asked[:, head * SLOT : (head + 1) * SLOT]

    def pass_on(step):
        for hop in range(1, half):
            along_ba(step, hop).start()
        to_partner(step, 0).start()

    def frame_step(step, first, with_queries):
        @pl.loop(1, half)
        def _(hop):
            landed(frame_of(step), (ba + n_ba - 2 * hop) % n_ba)
            to_partner(step, hop).start()

        @pl.when(step + 2 < n_aa)
        def _():
            landed(frame_of(step + 2), ba)
            pass_on(step + 2)

        @pl.loop(first, half)
        def _(hop):
            landed(frame_of(step), (partner + n_ba - 2 * hop) % n_ba)
            take_pair(step, hop, with_queries)

    for step in range(1, n_aa):
        along_aa(step).start()
    pass_on(0)
    sent(0)
    sent(1)
    landed(aa, partner)
    take_pair(0, 0, True)
    landed(frame_of(1), ba)
    pass_on(1)
    frame_step(0, 1, True)

    @pl.loop(1, n_aa)
    def _(step):
        frame_step(step, 0, False)

    for step in range(1, n_aa):
        along_aa(step).wait_send()

    @pl.loop(0, n_aa)
    def _(step):
        to_partner(step, 0).wait_send()

        @pl.loop(1, half)
        def _(hop):
            along_ba(step, hop).wait_send()
            to_partner(step, hop).wait_send()

    def share(dest):
        offset = (dest + n_ba - ba) % n_ba
        return pltpu.make_async_remote_copy(
            src_ref=shares.at[dest], dst_ref=arrived.at[ba],
            send_sem=share_send.at[offset], recv_sem=share_recv.at[offset],
            device_id=(aa, dest), device_id_type=MESH,
        )

    per_span = span // tokens
    spans = n_ba // per_span
    total = keys.shape[1]
    big = math.gcd(total, 4096)

    @pl.loop(0, spans)
    def _(step):
        at = (ba // per_span + 1 + step) % spans
        where = pl.ds(pl.multiple_of(at * span, span), span)

        def sweep(group, asked, base, state):
            order = [(each, part) for each in range(len(asked)) for part in range(big // chunk)]

            def held(part):
                return pl.ds(pl.multiple_of(base + part * chunk, chunk), chunk)

            def score(each, part):
                return lax.dot_general(
                    keys[group + each, held(part)], asked[each], (((1,), (1,)), ((), ())),
                    preferred_element_type=F32,
                )

            def gather(each, part, shrink, probs):
                best, accum = state[each]
                added = dot(values[group + each, :, held(part)], probs)
                return added if shrink is None else accum * shrink + added

            ahead = [score(*one) for one in order[:LOOK]]
            late = None
            for index, (each, part) in enumerate(order):
                if index + LOOK < len(order):
                    ahead.append(score(*order[index + LOOK]))
                scores, ahead[index] = ahead[index], None
                best, accum = state[each]
                peak = scores.max(0, keepdims=True)
                shrink = None
                if best is not None:
                    peak = jnp.maximum(best, peak)
                    shrink = jnp.exp2(best - peak)
                probs = jnp.exp2(scores - peak).astype(BF16)
                if late is not None:
                    state[late[0]] = (state[late[0]][0], gather(*late))
                state[each] = (peak, state[each][1])
                late = (each, part, shrink, probs)
            state[late[0]] = (state[late[0]][0], gather(*late))
            return state

        @pl.loop(0, heads // GROUP)
        def _(index):
            group = index * GROUP
            asked = [queries[group + each, where] for each in range(GROUP)]
            if total == big:
                state = sweep(group, asked, 0, [(None, None)] * GROUP)
            else:
                empty = (jnp.full((1, span), -jnp.inf, F32), jnp.zeros((values.shape[1], span), F32))

                def one_big(index, state):
                    return tuple(sweep(group, asked, index * big, list(state)))

                state = lax.fori_loop(0, total // big, one_big, (empty,) * GROUP)
            for each in range(GROUP):
                accum = state[each][1]
                rows = pl.ds(pl.multiple_of((group + each) * HEAD_DIM, HEAD_DIM), HEAD_DIM)
                attended[rows] = (accum[:HEAD_DIM] / accum[HEAD_DIM : HEAD_DIM + 1]).astype(BF16)

        velocity = lax.dot_general(
            w_velocity[...], attended[...], (((0,), (0,)), ((), ())), preferred_element_type=F32
        )
        for part in range(per_span):
            dest = at * per_span + part
            shares[dest] = velocity[:, part * tokens : (part + 1) * tokens].astype(BF16)

            @pl.when(dest != ba)
            def _():
                share(dest).start()

    summed = shares[ba].astype(F32)
    for offset in range(1, n_ba):
        share((ba + offset) % n_ba).wait_recv()
        summed += arrived[(ba + n_ba - offset) % n_ba].astype(F32)
    out[...] = summed.T
    for offset in range(1, n_ba):
        share((ba + offset) % n_ba).wait_send()


def on_device(
    n_aa, n_ba,
    feats, conv_one, bias_one, conv_two, bias_two, patch_weight, patch_bias,
    embed_weight, embed_bias, norm_gain, w_query, w_key, w_value, w_velocity,
):
    _, rows, width, chans = feats.shape
    lat = patch_bias.shape[0]
    features, qwidth = w_query.shape
    heads = qwidth // HEAD_DIM
    tokens = rows * width // 4
    total = n_ba * n_aa * tokens
    span = max(tokens, min(512, n_ba * tokens))
    chunk = math.gcd(total, 256)
    vmem = pl.BlockSpec(memory_space=pltpu.VMEM)
    anywhere = pl.BlockSpec(memory_space=pl.ANY)
    dma = pltpu.SemaphoreType.DMA
    return pl.pallas_call(
        functools.partial(whole_kernel, n_aa, n_ba, span, chunk),
        out_shape=jax.ShapeDtypeStruct((tokens, lat), F32),
        in_specs=[anywhere, anywhere, vmem, anywhere] + [vmem] * 6 + [anywhere] * 3 + [vmem],
        out_specs=vmem,
        scratch_shapes=[
            pltpu.VMEM((2, 3, rows + 2, width, chans), BF16),
            pltpu.VMEM((2, 9, chans, 3 * chans), BF16),
            pltpu.VMEM((3, features, qwidth), BF16),
            pltpu.VMEM((2, 2, rows, width, chans), BF16),
            pltpu.VMEM((2, 2, rows, width, chans), BF16),
            pltpu.VMEM((rows, width, chans), F32),
            pltpu.VMEM((2, width, lat), F32),
            pltpu.VMEM((n_aa, n_ba, tokens, lat), BF16),
            pltpu.VMEM((2, 2 * lat, heads * SLOT), BF16),
            pltpu.VMEM((2, 8, heads * SLOT), F32),
            pltpu.VMEM((qwidth + 2 * lat, 2 * lat), BF16),
            pltpu.VMEM((qwidth, 8), F32),
            pltpu.VMEM((2 * lat, lat), BF16),
            pltpu.VMEM((lat + 8, lat + 8), F32),
            pltpu.VMEM((heads, n_ba * tokens, SLOT), BF16),
            pltpu.VMEM((heads, total, SLOT), BF16),
            pltpu.VMEM((heads, STACK, total), BF16),
            pltpu.VMEM((qwidth, span), BF16),
            pltpu.VMEM((n_ba, lat, tokens), BF16),
            pltpu.VMEM((n_ba, lat, tokens), BF16),
            dma((10,)),
            dma((2, 2, 2)), dma((2, 2, 2)), dma((2, 2)), dma((2, 2)),
            dma((n_aa, n_ba)), dma((n_aa,)), dma((n_aa, n_ba // 2)), dma((n_aa, n_ba // 2)),
            dma((n_ba,)), dma((n_ba,)),
        ],
        compiler_params=pltpu.CompilerParams(
            collective_id=0, has_side_effects=True, vmem_limit_bytes=VMEM_BYTES
        ),
        name="whole",
    )(
        feats, conv_one.reshape(3, 9, chans, chans), bias_one[None],
        conv_two.reshape(3, 9, chans, chans), bias_two[None],
        patch_weight, patch_bias[None], embed_weight, embed_bias[None], norm_gain[None],
        w_query, w_key, w_value, w_velocity,
    )


def solution(mesh):
    return jax.shard_map(
        functools.partial(on_device, mesh.shape["aa"], mesh.shape["ba"]),
        mesh=mesh,
        in_specs=(
            P("aa", "ba", None, None), P(), P(), P(), P(), P(), P(), P(), P(), P(),
            P(None, "ba"), P(None, "ba"), P(None, "ba"), P("ba", None),
        ),
        out_specs=P(("aa", "ba"), None),
        check_vma=False,
    )
```

```python
import functools
import math

import jax
import jax.numpy as jnp
from jax import lax
from jax.experimental import pallas as pl
from jax.experimental.pallas import tpu as pltpu
from jax.sharding import PartitionSpec as P

HEAD_DIM = 64
SLOT = 128
MESH = pl.DeviceIdType.MESH
GROUP = 2
LOOK = 2
STACK = HEAD_DIM + 16
F32 = jnp.float32
BF16 = jnp.bfloat16
VMEM_BYTES = 67043328


def dot(left, right):
    return jnp.dot(left, right, preferred_element_type=F32)


def two_parts(value):
    high = value.astype(BF16)
    return high, (value - high.astype(F32)).astype(BF16)


def gelu(value):
    return 0.5 * value * (1.0 + lax.erf(value * (0.5**0.5)))


def whole_kernel(
    n_aa, n_ba, span, narrow, chunk,
    feats, conv_one, bias_one_in, conv_two, bias_two_in, patch_weight_in, patch_bias_in,
    embed_weight_in, embed_bias_in, norm_gain_in, w_query, w_key, w_value, w_velocity_in,
    out,
    bias_one, bias_two, patch_weight, patch_bias, embed_weight, embed_bias, norm_gain, w_velocity, gained,
    field, taps, w_joined, outgoing, incoming, acc, pair, gathered, split_query, query_offset, split_key, key_offset, turned, lift,
    gram_split, gram, queries, keys, values, attended, shares, arrived,
    load_sem, small_sem, aa_side_send, aa_side_recv, ba_side_send, ba_side_recv,
    token_recv, aa_send, ba_send, core_send, share_send, share_recv,
):
    aa, ba = lax.axis_index("aa"), lax.axis_index("ba")
    _, rows, width, chans = feats.shape
    partner = ba + 1 - 2 * (ba % 2)
    half = n_ba // 2
    width_q = w_query.shape[1]
    heads = width_q // HEAD_DIM
    tokens = rows * width // 4
    lat = patch_bias.shape[1]

    def load(source, target, at):
        return pltpu.make_async_copy(source, target, load_sem.at[at])

    loads = [
        load(feats.at[0], field.at[0, 1, pl.ds(1, rows)], 0),
        load(w_query, w_joined.at[0], 1),
        load(w_key, w_joined.at[1], 2),
        load(w_value, w_joined.at[2], 3),
    ]
    kernels = [
        [load(source.at[at], taps.at[which, :, :, pl.ds(column * chans, chans)], 4 + 3 * which + at)
         for at, column in enumerate((0, 2, 1))]
        for which, source in enumerate((conv_one, conv_two))
    ]
    small = [
        pltpu.make_async_copy(source, target, small_sem.at[at])
        for at, (source, target) in enumerate((
            (bias_one_in, bias_one), (embed_weight_in, embed_weight), (embed_bias_in, embed_bias),
            (norm_gain_in, norm_gain), (bias_two_in, bias_two), (patch_weight_in, patch_weight),
            (patch_bias_in, patch_bias), (w_velocity_in, w_velocity),
        ))
    ]
    loads[0].start()
    for at in (0, 2, 1):
        kernels[0][at].start()
    for one in small[:4]:
        one.start()
    for one in loads[1:]:
        one.start()
    for at in (0, 2, 1):
        kernels[1][at].start()
    for one in small[4:]:
        one.start()

    def aa_there(side):
        return aa > 0 if side == -1 else aa < n_aa - 1

    def ba_there(side):
        return ba > 0 if side == -1 else ba < n_ba - 1

    barrier = pltpu.get_barrier_semaphore()
    for step in range(1, n_aa):
        pl.semaphore_signal(
            barrier, inc=1, device_id=((aa + step) % n_aa, ba), device_id_type=MESH
        )
    for step in range(1, n_ba):
        pl.semaphore_signal(
            barrier, inc=1, device_id=(aa, (ba + step) % n_ba), device_id_type=MESH
        )

    edges, middle, both = 0, 1, 2
    parts = (slice(0, 2), slice(2, rows))

    def along_time(which, side, part):
        at = (which, (side + 1) // 2, part)
        here = (which, (side + 1) // 2, parts[part])
        return pltpu.make_async_remote_copy(
            src_ref=outgoing.at[here], dst_ref=incoming.at[here],
            send_sem=aa_side_send.at[at], recv_sem=aa_side_recv.at[at],
            device_id=(aa + side, ba), device_id_type=MESH,
        )

    def along_rows(which, side):
        source, target = (rows, 0) if side == 1 else (1, rows + 1)
        at = (which, (side + 1) // 2)
        return pltpu.make_async_remote_copy(
            src_ref=field.at[which, 1, source], dst_ref=field.at[which, 1, target],
            send_sem=ba_side_send.at[at], recv_sem=ba_side_recv.at[at],
            device_id=(aa, ba + side), device_id_type=MESH,
        )

    def send_rows(which):
        for side in (-1, 1):
            pl.when(ba_there(side))(along_rows(which, side).start)

    def take_rows(which):
        for side in (-1, 1):
            pl.when(ba_there(-side))(along_rows(which, side).wait_recv)
        shift(which, 0, 1)
        shift(which, rows + 1, 1)

    def take_time(which, part):
        for side in (-1, 1):
            pl.when(aa_there(-side))(along_time(which, side, part).wait_recv)

    def sent(which):
        for side in (-1, 1):
            pl.when(ba_there(side))(along_rows(which, side).wait_send)
            for part in (edges, middle):
                pl.when(aa_there(side))(along_time(which, side, part).wait_send)

    def blank():
        line = jnp.zeros((width, chans), BF16)
        for which in range(2):
            for side, row in ((-1, 0), (1, rows + 1)):
                @pl.when(jnp.logical_not(ba_there(side)))
                def _():
                    field[which, 1, row] = line

                @pl.when(jnp.logical_not(aa_there(side)))
                def _():
                    for at in range(rows):
                        incoming[which, (1 - side) // 2, at] = line

    def shift(which, row, count):
        here = pl.ds(row, count)
        held = field[which, 1, here].reshape(count * width, chans).astype(F32)
        place = lax.broadcasted_iota(jnp.int32, held.shape, 0) % width
        before = jnp.where(place == 0, 0.0, pltpu.roll(held, 1, 0))
        after = jnp.where(place == width - 1, 0.0, pltpu.roll(held, count * width - 1, 0))
        field[which, 0, here] = before.astype(BF16).reshape(count, width, chans)
        field[which, 2, here] = after.astype(BF16).reshape(count, width, chans)

    def stack(which, part):
        def window(shift_r, shift_w):
            if part == middle:
                held = field[which, shift_w, pl.ds(1 + shift_r, rows - 2)]
                return held.reshape((rows - 2) * width, chans)
            if part == both:
                return field[which, shift_w, pl.ds(shift_r, rows)].reshape(rows * width, chans)
            return jnp.concatenate(
                [field[which, shift_w, shift_r], field[which, shift_w, rows - 1 + shift_r]], axis=0
            )

        return jnp.concatenate(
            [window(shift_r, shift_w) for shift_r in range(3) for shift_w in range(3)], axis=1
        )

    def send_time(which, part):
        made = dot(
            stack(which, part), taps[which, :, :, : 2 * chans].reshape(9 * chans, 2 * chans)
        ).astype(BF16)
        for side, column in ((-1, chans), (1, 0)):
            outgoing[which, (side + 1) // 2, parts[part]] = made[
                :, column : column + chans
            ].reshape(-1, width, chans)
            pl.when(aa_there(side))(along_time(which, side, part).start)

    def keep(which):
        acc[...] = dot(
            stack(which, both), taps[which, :, :, 2 * chans :].reshape(9 * chans, chans)
        ).reshape(rows, width, chans)

    def activate(which, part, bias):
        here = parts[part]
        kept = acc[1 : rows - 1] if part == middle else jnp.concatenate(
            [acc[:1], acc[rows - 1 :]], axis=0
        )
        total = kept + incoming[which, 0, here].astype(F32)
        total += incoming[which, 1, here].astype(F32)
        return gelu(total.reshape(-1, chans) + bias)

    blank()
    loads[0].wait()
    shift(0, 1, rows)
    pl.semaphore_wait(barrier, n_aa - 1 + n_ba - 1)
    send_rows(0)
    kernels[0][0].wait()
    kernels[0][2].wait()
    send_time(0, middle)
    take_rows(0)
    send_time(0, edges)

    def merge_gram():
        for one in small[:4]:
            one.wait()
        embed = embed_weight[...].astype(F32)
        centred = jnp.concatenate(
            [
                embed - embed.mean(-1, keepdims=True),
                jnp.broadcast_to(
                    embed_bias[...] - embed_bias[...].mean(-1, keepdims=True),
                    (8, embed.shape[1]),
                ),
            ],
            axis=0,
        )
        gram[...] = lax.dot_general(
            centred, centred, (((1,), (1,)), ((), ())),
            precision=lax.Precision.HIGHEST, preferred_element_type=F32,
        ) * (1.0 / embed.shape[1])
        high, low = two_parts(gram[:lat, :lat])
        gram_split[:lat] = high
        gram_split[lat:] = low
        turned[width_q : width_q + lat, :lat] = high
        turned[width_q : width_q + lat, lat:] = low
        across = lax.broadcasted_iota(jnp.int32, (lat, 2 * lat), 1)
        down = lax.broadcasted_iota(jnp.int32, (lat, 2 * lat), 0)
        turned[width_q + lat :] = (across == down).astype(BF16)
        gained[...] = jnp.concatenate(two_parts(centred * norm_gain[...]), axis=0)

    def merge(which):
        loads[1 + which].wait()
        product = dot(gained[...], w_joined[which])
        product = product[: lat + 8] + product[lat + 8 :]
        if which == 0:
            product = product * (HEAD_DIM**-0.5 * math.log2(math.e))
            blanks = jnp.zeros((product.shape[0], HEAD_DIM), F32)
            for head in range(heads):
                piece = product[:, head * HEAD_DIM : (head + 1) * HEAD_DIM]
                ordered = (blanks, piece) if head % 2 else (piece, blanks)
                piece = jnp.concatenate(ordered, axis=1)
                slot = slice(head * SLOT, (head + 1) * SLOT)
                high, low = two_parts(piece[:lat])
                split_query[:lat, slot] = high
                split_query[lat:, slot] = low
                query_offset[:, slot] = piece[lat:]
        elif which == 1:
            high, low = two_parts(product[:lat])
            split_key[:lat] = high
            split_key[lat:] = low
            key_offset[...] = product[lat:]
        else:
            high, low = two_parts(product[:lat].T)
            turned[:width_q, :lat] = high
            turned[:width_q, lat:] = low
            lift[...] = product[lat:].T

    kernels[0][1].wait()
    keep(0)
    merge_gram()
    merge(2)
    take_time(0, middle)
    first = activate(0, middle, bias_one[...]).astype(BF16)
    field[1, 1, 2:rows] = first.reshape(-1, width, chans)
    shift(1, 2, rows - 2)
    take_time(0, edges)
    first = activate(0, edges, bias_one[...]).astype(BF16)
    field[1, 1, 1] = first[:width]
    field[1, 1, rows] = first[width:]
    send_rows(1)
    shift(1, 1, 1)
    shift(1, rows, 1)
    for at in (0, 2, 1):
        kernels[1][at].wait()
    send_time(1, middle)
    merge(1)
    take_rows(1)
    send_time(1, edges)
    keep(1)
    merge(0)
    for one in small[4:]:
        one.wait()

    def finish(part):
        here = field[1, 1, 2:rows] if part == middle else jnp.concatenate(
            [field[1, 1, 1], field[1, 1, rows]], axis=0
        )
        own = here.reshape(-1, chans).astype(F32)
        return (own + activate(1, part, bias_two[...])).astype(BF16)

    take_time(1, middle)
    inner = finish(middle)
    take_time(1, edges)
    outer = finish(edges)
    lines = [outer[:width]]
    lines += [inner[at * width : (at + 1) * width] for at in range(rows - 2)]
    lines += [outer[width:]]

    line = width // 2
    for block in range(rows // 2):
        for col in range(2):
            pair[col] = dot(lines[2 * block], patch_weight[0, col]) + dot(
                lines[2 * block + 1], patch_weight[1, col]
            )
        patches = (
            pair[0, pl.ds(0, line, stride=2), :] + pair[1, pl.ds(1, line, stride=2), :]
            + patch_bias[...]
        ).astype(BF16)
        gathered[aa, ba, pl.ds(block * line, line), :] = patches

    values[:, HEAD_DIM:] = jnp.ones((heads, values.shape[1] - HEAD_DIM, values.shape[2]), BF16)

    flanked = jnp.minimum(aa, n_aa - 1 - aa)
    toward = jnp.where(aa < n_aa - 1 - aa, 1, -1)

    def frame_of(step):
        near = (1 - 2 * ((step + 1) % 2)) * ((step + 1) // 2)
        return aa + jnp.where(step <= 2 * flanked, near, toward * (step - flanked))

    def piece(frame, block, send_sem, to_aa, to_ba):
        here = gathered.at[frame, block]
        return pltpu.make_async_remote_copy(
            src_ref=here, dst_ref=here, send_sem=send_sem, recv_sem=token_recv.at[frame, block],
            device_id=(to_aa, to_ba), device_id_type=MESH,
        )

    def along_aa(step):
        return piece(aa, ba, aa_send.at[step], frame_of(step), ba)

    def along_ba(step, hop):
        return piece(frame_of(step), ba, ba_send.at[step, hop], aa, (ba + 2 * hop) % n_ba)

    def to_partner(step, hop):
        block = (ba + n_ba - 2 * hop) % n_ba
        return piece(frame_of(step), block, core_send.at[step, hop], aa, partner)

    def landed(frame, block):
        piece(frame, block, aa_send.at[0], aa, partner).wait_recv()

    slope = 2.0 * gram[lat : lat + 1, :lat]
    slope_down = 2.0 * gram[:lat, lat : lat + 1]
    floor = gram[lat : lat + 1, lat : lat + 1]

    def take_pairs(step, hops, with_queries):
        frame = frame_of(step)
        blocks = [((ba + n_ba - 2 * hop) % n_ba) // 2 for hop in hops]
        size = 2 * tokens
        latents = jnp.concatenate(
            [gathered[frame, pl.ds(2 * block, 2)].reshape(size, lat) for block in blocks], axis=0
        )
        twice = jnp.concatenate([latents, latents], axis=1)
        bent = dot(twice, gram_split[...]) + slope
        power = (bent * latents.astype(F32)).sum(-1, keepdims=True) + floor
        scale = lax.rsqrt(jnp.maximum(power, 0.0) + 1e-05)
        projected = ((dot(twice, split_key[...]) + key_offset[:1]) * scale).astype(BF16)
        down = lax.dot_general(
            turned[...], twice, (((1,), (1,)), ((), ())), preferred_element_type=F32
        )
        bent = (down[width_q : width_q + lat] + slope_down) * down[width_q + lat :]
        power = bent.sum(0, keepdims=True) + floor
        scale_down = lax.rsqrt(jnp.maximum(power, 0.0) + 1e-05)
        flipped = ((down[:width_q] + lift[:, :1]) * scale_down).astype(BF16)
        for index, block in enumerate(blocks):
            own = slice(index * size, (index + 1) * size)
            at = pl.ds(pl.multiple_of((frame * half + block) * size, size), size)
            for couple in range(heads // 2):
                keys[couple, at] = projected[own, couple * SLOT : (couple + 1) * SLOT]
            for head in range(heads):
                values[head, :HEAD_DIM, at] = flipped[head * HEAD_DIM : (head + 1) * HEAD_DIM, own]
        if with_queries:
            asked = ((dot(twice, split_query[...]) + query_offset[:1]) * scale).astype(BF16)
            for index, block in enumerate(blocks):
                own = slice(index * size, (index + 1) * size)
                there = pl.ds(pl.multiple_of(block * size, size), size)
                for head in range(heads):
                    queries[head, there] = asked[own, head * SLOT : (head + 1) * SLOT]

    def pass_on(step):
        for hop in range(1, half):
            along_ba(step, hop).start()
        to_partner(step, 0).start()

    def advance(step):
        landed(frame_of(step), ba)
        pass_on(step)

    def hand_over(step):
        @pl.loop(1, half)
        def _(hop):
            landed(frame_of(step), (ba + n_ba - 2 * hop) % n_ba)
            to_partner(step, hop).start()

    def take(step, hop, with_queries):
        landed(frame_of(step), (partner + n_ba - 2 * hop) % n_ba)
        take_pairs(step, [hop], with_queries)

    def take_rest(step, with_queries):
        @pl.loop(1, half)
        def _(hop):
            take(step, hop, with_queries)

    for step in range(1, n_aa):
        along_aa(step).start()
    pass_on(0)
    sent(0)
    sent(1)
    take(0, 0, True)
    advance(1)
    hand_over(0)

    @pl.loop(1, half)
    def _(hop):
        take(0, hop, True)
        pl.when(hop + 1 < n_aa)(lambda: advance(hop + 1))

    for step in range(half + 1, n_aa):
        advance(step)
    hand_over(1)
    take(1, 0, False)

    @pl.loop(2, n_aa)
    def _(step):
        hand_over(step)
        take_rest(step - 1, False)
        take(step, 0, False)

    take_rest(n_aa - 1, False)

    for step in range(1, n_aa):
        along_aa(step).wait_send()

    @pl.loop(0, n_aa)
    def _(step):
        to_partner(step, 0).wait_send()

        @pl.loop(1, half)
        def _(hop):
            along_ba(step, hop).wait_send()
            to_partner(step, hop).wait_send()

    def share(dest):
        offset = (dest + n_ba - ba) % n_ba
        return pltpu.make_async_remote_copy(
            src_ref=shares.at[dest], dst_ref=arrived.at[ba],
            send_sem=share_send.at[offset], recv_sem=share_recv.at[offset],
            device_id=(aa, dest), device_id_type=MESH,
        )

    total = keys.shape[1]
    big = math.gcd(total, 4096)

    def attend(at, span, chunk):
        per_span = span // tokens
        where = pl.ds(pl.multiple_of(at * span, span), span)

        def sweep(group, asked, base, state):
            order = [(each, part) for each in range(len(asked)) for part in range(big // chunk)]

            def held(part):
                return pl.ds(pl.multiple_of(base + part * chunk, chunk), chunk)

            def score(each, part):
                return lax.dot_general(
                    keys[(group + each) // 2, held(part)], asked[each], (((1,), (1,)), ((), ())),
                    preferred_element_type=F32,
                )

            def gather(each, part, shrink, probs):
                best, accum = state[each]
                added = dot(values[group + each, :, held(part)], probs)
                return added if shrink is None else accum * shrink + added

            ahead = [score(*one) for one in order[:LOOK]]
            late = None
            for index, (each, part) in enumerate(order):
                if index + LOOK < len(order):
                    ahead.append(score(*order[index + LOOK]))
                scores, ahead[index] = ahead[index], None
                best, accum = state[each]
                peak = scores.max(0, keepdims=True)
                shrink = None
                if best is not None:
                    peak = jnp.maximum(best, peak)
                    shrink = jnp.exp2(best - peak)
                probs = jnp.exp2(scores - peak).astype(BF16)
                if late is not None:
                    state[late[0]] = (state[late[0]][0], gather(*late))
                state[each] = (peak, state[each][1])
                late = (each, part, shrink, probs)
            state[late[0]] = (state[late[0]][0], gather(*late))
            return state

        @pl.loop(0, heads // GROUP)
        def _(index):
            group = index * GROUP
            asked = [queries[group + each, where] for each in range(GROUP)]
            if total == big:
                state = sweep(group, asked, 0, [(None, None)] * GROUP)
            else:
                empty = (jnp.full((1, span), -jnp.inf, F32), jnp.zeros((values.shape[1], span), F32))

                def one_big(index, state):
                    return tuple(sweep(group, asked, index * big, list(state)))

                state = lax.fori_loop(0, total // big, one_big, (empty,) * GROUP)
            for each in range(GROUP):
                accum = state[each][1]
                rows = pl.ds(pl.multiple_of((group + each) * HEAD_DIM, HEAD_DIM), HEAD_DIM)
                attended[rows, :span] = (accum[:HEAD_DIM] / accum[HEAD_DIM : HEAD_DIM + 1]).astype(BF16)

        velocity = lax.dot_general(
            w_velocity[...], attended[:, :span], (((0,), (0,)), ((), ())), preferred_element_type=F32
        )
        for part in range(per_span):
            dest = at * per_span + part
            shares[dest] = velocity[:, part * tokens : (part + 1) * tokens].astype(BF16)

            @pl.when(dest != ba)
            def _():
                share(dest).start()

    wide = n_ba * tokens // span
    fine = span // narrow
    mine = ba * tokens // span

    @pl.loop(1, wide)
    def _(step):
        attend((mine + step) % wide, span, chunk)

    @pl.loop(1, fine + 1)
    def _(step):
        attend(mine * fine + (ba * tokens // narrow + step) % fine, narrow, 2 * chunk)

    summed = shares[ba].astype(F32)
    for offset in range(1, n_ba):
        share((ba + offset) % n_ba).wait_recv()
        summed += arrived[(ba + n_ba - offset) % n_ba].astype(F32)
    out[...] = summed.T
    for offset in range(1, n_ba):
        share((ba + offset) % n_ba).wait_send()


def on_device(
    n_aa, n_ba,
    feats, conv_one, bias_one, conv_two, bias_two, patch_weight, patch_bias,
    embed_weight, embed_bias, norm_gain, w_query, w_key, w_value, w_velocity,
):
    _, rows, width, chans = feats.shape
    lat = patch_bias.shape[0]
    features, qwidth = w_query.shape
    heads = qwidth // HEAD_DIM
    tokens = rows * width // 4
    total = n_ba * n_aa * tokens
    span = max(tokens, min(512, n_ba * tokens))
    narrow = max(tokens, min(256, span))
    chunk = math.gcd(total, 256)
    vmem = pl.BlockSpec(memory_space=pltpu.VMEM)
    anywhere = pl.BlockSpec(memory_space=pl.ANY)
    dma = pltpu.SemaphoreType.DMA
    return pl.pallas_call(
        functools.partial(whole_kernel, n_aa, n_ba, span, narrow, chunk),
        out_shape=jax.ShapeDtypeStruct((tokens, lat), F32),
        in_specs=[anywhere] * 14,
        out_specs=vmem,
        scratch_shapes=[
            pltpu.VMEM((1, chans), F32),
            pltpu.VMEM((1, chans), F32),
            pltpu.VMEM((2, 2, chans, lat), BF16),
            pltpu.VMEM((1, lat), F32),
            pltpu.VMEM((lat, features), BF16),
            pltpu.VMEM((1, features), F32),
            pltpu.VMEM((1, features), F32),
            pltpu.VMEM((qwidth, lat), BF16),
            pltpu.VMEM((2 * lat + 16, features), BF16),
            pltpu.VMEM((2, 3, rows + 2, width, chans), BF16),
            pltpu.VMEM((2, 9, chans, 3 * chans), BF16),
            pltpu.VMEM((3, features, qwidth), BF16),
            pltpu.VMEM((2, 2, rows, width, chans), BF16),
            pltpu.VMEM((2, 2, rows, width, chans), BF16),
            pltpu.VMEM((rows, width, chans), F32),
            pltpu.VMEM((2, width, lat), F32),
            pltpu.VMEM((n_aa, n_ba, tokens, lat), BF16),
            pltpu.VMEM((2 * lat, heads * SLOT), BF16),
            pltpu.VMEM((8, heads * SLOT), F32),
            pltpu.VMEM((2 * lat, qwidth), BF16),
            pltpu.VMEM((8, qwidth), F32),
            pltpu.VMEM((qwidth + 2 * lat, 2 * lat), BF16),
            pltpu.VMEM((qwidth, 8), F32),
            pltpu.VMEM((2 * lat, lat), BF16),
            pltpu.VMEM((lat + 8, lat + 8), F32),
            pltpu.VMEM((heads, n_ba * tokens, SLOT), BF16),
            pltpu.VMEM((heads // 2, total, SLOT), BF16),
            pltpu.VMEM((heads, STACK, total), BF16),
            pltpu.VMEM((qwidth, span), BF16),
            pltpu.VMEM((n_ba, lat, tokens), BF16),
            pltpu.VMEM((n_ba, lat, tokens), BF16),
            dma((10,)), dma((8,)),
            dma((2, 2, 2)), dma((2, 2, 2)), dma((2, 2)), dma((2, 2)),
            dma((n_aa, n_ba)), dma((n_aa,)), dma((n_aa, n_ba // 2)), dma((n_aa, n_ba // 2)),
            dma((n_ba,)), dma((n_ba,)),
        ],
        compiler_params=pltpu.CompilerParams(
            collective_id=0, has_side_effects=True, vmem_limit_bytes=VMEM_BYTES
        ),
        name="whole",
    )(
        feats, conv_one.reshape(3, 9, chans, chans), bias_one[None],
        conv_two.reshape(3, 9, chans, chans), bias_two[None],
        patch_weight, patch_bias[None], embed_weight, embed_bias[None], norm_gain[None],
        w_query, w_key, w_value, w_velocity,
    )


def solution(mesh):
    return jax.shard_map(
        functools.partial(on_device, mesh.shape["aa"], mesh.shape["ba"]),
        mesh=mesh,
        in_specs=(
            P("aa", "ba", None, None), P(), P(), P(), P(), P(), P(), P(), P(), P(),
            P(None, "ba"), P(None, "ba"), P(None, "ba"), P("ba", None),
        ),
        out_specs=P(("aa", "ba"), None),
        check_vma=False,
    )
```

```python
import functools
import math

import jax
import jax.numpy as jnp
from jax import lax
from jax.experimental import pallas as pl
from jax.experimental.pallas import tpu as pltpu
from jax.sharding import PartitionSpec as P

HEAD_DIM = 64
SLOT = 128
MESH = pl.DeviceIdType.MESH
LOOK = 1
GROUPED = 4
STACK = HEAD_DIM + 16
F32 = jnp.float32
BF16 = jnp.bfloat16
VMEM_BYTES = 67043328


def dot(left, right):
    return jnp.dot(left, right, preferred_element_type=F32)


def two_parts(value):
    high = value.astype(BF16)
    return high, (value - high.astype(F32)).astype(BF16)


def gelu(value):
    return 0.5 * value * (1.0 + lax.erf(value * (0.5**0.5)))


def whole_kernel(
    n_aa, n_ba, span, chunk,
    feats, conv_one, bias_one_in, conv_two, bias_two_in, patch_weight_in, patch_bias_in,
    embed_weight_in, embed_bias_in, norm_gain_in, w_query, w_key, w_value, w_velocity_in,
    out,
    bias_one, bias_two, patch_weight, patch_bias, embed_weight, embed_bias, norm_gain, w_velocity, gained,
    field, taps, w_joined, outgoing, incoming, acc, pair, gathered, turned_query, query_lift, split_key, key_offset, turned, lift,
    gram_split, gram, queries, keys, values, attended, shares, arrived,
    load_sem, small_sem, aa_side_send, aa_side_recv, ba_side_send, ba_side_recv,
    token_recv, aa_send, ba_send, core_send, share_send, share_recv,
):
    aa, ba = lax.axis_index("aa"), lax.axis_index("ba")
    _, rows, width, chans = feats.shape
    partner = ba + 1 - 2 * (ba % 2)
    half = n_ba // 2
    width_q = w_query.shape[1]
    heads = width_q // HEAD_DIM
    group_size = math.gcd(heads, GROUPED)
    tokens = rows * width // 4
    lat = patch_bias.shape[1]

    def load(source, target, at):
        return pltpu.make_async_copy(source, target, load_sem.at[at])

    loads = [
        load(feats.at[0], field.at[0, 1, pl.ds(1, rows)], 0),
        load(w_query, w_joined.at[0], 1),
        load(w_key, w_joined.at[1], 2),
        load(w_value, w_joined.at[2], 3),
    ]
    kernels = [
        [load(source.at[at], taps.at[which, :, :, pl.ds(column * chans, chans)], 4 + 3 * which + at)
         for at, column in enumerate((0, 2, 1))]
        for which, source in enumerate((conv_one, conv_two))
    ]
    small = [
        pltpu.make_async_copy(source, target, small_sem.at[at])
        for at, (source, target) in enumerate((
            (bias_one_in, bias_one), (embed_weight_in, embed_weight), (embed_bias_in, embed_bias),
            (norm_gain_in, norm_gain), (bias_two_in, bias_two), (patch_weight_in, patch_weight),
            (patch_bias_in, patch_bias), (w_velocity_in, w_velocity),
        ))
    ]
    loads[0].start()
    for at in (0, 2, 1):
        kernels[0][at].start()
    for one in small[:4]:
        one.start()
    for one in loads[1:]:
        one.start()
    for at in (0, 2, 1):
        kernels[1][at].start()
    for one in small[4:]:
        one.start()

    def aa_there(side):
        return aa > 0 if side == -1 else aa < n_aa - 1

    def ba_there(side):
        return ba > 0 if side == -1 else ba < n_ba - 1

    barrier = pltpu.get_barrier_semaphore()
    for step in range(1, n_aa):
        pl.semaphore_signal(
            barrier, inc=1, device_id=((aa + step) % n_aa, ba), device_id_type=MESH
        )
    for step in range(1, n_ba):
        pl.semaphore_signal(
            barrier, inc=1, device_id=(aa, (ba + step) % n_ba), device_id_type=MESH
        )

    edges, middle, both = 0, 1, 2
    parts = (slice(0, 2), slice(2, rows))

    def along_time(which, side, part):
        at = (which, (side + 1) // 2, part)
        here = (which, (side + 1) // 2, parts[part])
        return pltpu.make_async_remote_copy(
            src_ref=outgoing.at[here], dst_ref=incoming.at[here],
            send_sem=aa_side_send.at[at], recv_sem=aa_side_recv.at[at],
            device_id=(aa + side, ba), device_id_type=MESH,
        )

    def along_rows(which, side):
        source, target = (rows, 0) if side == 1 else (1, rows + 1)
        at = (which, (side + 1) // 2)
        return pltpu.make_async_remote_copy(
            src_ref=field.at[which, 1, source], dst_ref=field.at[which, 1, target],
            send_sem=ba_side_send.at[at], recv_sem=ba_side_recv.at[at],
            device_id=(aa, ba + side), device_id_type=MESH,
        )

    def send_rows(which):
        for side in (-1, 1):
            pl.when(ba_there(side))(along_rows(which, side).start)

    def take_rows(which):
        for side in (-1, 1):
            pl.when(ba_there(-side))(along_rows(which, side).wait_recv)
        shift(which, 0, 1)
        shift(which, rows + 1, 1)

    def take_time(which, part):
        for side in (-1, 1):
            pl.when(aa_there(-side))(along_time(which, side, part).wait_recv)

    def sent(which):
        for side in (-1, 1):
            pl.when(ba_there(side))(along_rows(which, side).wait_send)
            for part in (edges, middle):
                pl.when(aa_there(side))(along_time(which, side, part).wait_send)

    def blank():
        line = jnp.zeros((width, chans), BF16)
        for which in range(2):
            for side, row in ((-1, 0), (1, rows + 1)):
                @pl.when(jnp.logical_not(ba_there(side)))
                def _():
                    field[which, 1, row] = line

                @pl.when(jnp.logical_not(aa_there(side)))
                def _():
                    for at in range(rows):
                        incoming[which, (1 - side) // 2, at] = line

    def shift(which, row, count):
        here = pl.ds(row, count)
        held = field[which, 1, here].reshape(count * width, chans).astype(F32)
        place = lax.broadcasted_iota(jnp.int32, held.shape, 0) % width
        before = jnp.where(place == 0, 0.0, pltpu.roll(held, 1, 0))
        after = jnp.where(place == width - 1, 0.0, pltpu.roll(held, count * width - 1, 0))
        field[which, 0, here] = before.astype(BF16).reshape(count, width, chans)
        field[which, 2, here] = after.astype(BF16).reshape(count, width, chans)

    def stack(which, part):
        def window(shift_r, shift_w):
            if part == middle:
                held = field[which, shift_w, pl.ds(1 + shift_r, rows - 2)]
                return held.reshape((rows - 2) * width, chans)
            if part == both:
                return field[which, shift_w, pl.ds(shift_r, rows)].reshape(rows * width, chans)
            return jnp.concatenate(
                [field[which, shift_w, shift_r], field[which, shift_w, rows - 1 + shift_r]], axis=0
            )

        return jnp.concatenate(
            [window(shift_r, shift_w) for shift_r in range(3) for shift_w in range(3)], axis=1
        )

    def send_time(which, part):
        made = dot(
            stack(which, part), taps[which, :, :, : 2 * chans].reshape(9 * chans, 2 * chans)
        ).astype(BF16)
        for side, column in ((-1, chans), (1, 0)):
            outgoing[which, (side + 1) // 2, parts[part]] = made[
                :, column : column + chans
            ].reshape(-1, width, chans)
            pl.when(aa_there(side))(along_time(which, side, part).start)

    def keep(which):
        acc[...] = dot(
            stack(which, both), taps[which, :, :, 2 * chans :].reshape(9 * chans, chans)
        ).reshape(rows, width, chans)

    def activate(which, part, bias):
        here = parts[part]
        kept = acc[1 : rows - 1] if part == middle else jnp.concatenate(
            [acc[:1], acc[rows - 1 :]], axis=0
        )
        total = kept + incoming[which, 0, here].astype(F32)
        total += incoming[which, 1, here].astype(F32)
        return gelu(total.reshape(-1, chans) + bias)

    blank()
    loads[0].wait()
    shift(0, 1, rows)
    pl.semaphore_wait(barrier, n_aa - 1 + n_ba - 1)
    send_rows(0)
    kernels[0][0].wait()
    kernels[0][2].wait()
    send_time(0, middle)
    take_rows(0)
    send_time(0, edges)

    def merge_gram():
        for one in small[:4]:
            one.wait()
        embed = embed_weight[...].astype(F32)
        centred = jnp.concatenate(
            [
                embed - embed.mean(-1, keepdims=True),
                jnp.broadcast_to(
                    embed_bias[...] - embed_bias[...].mean(-1, keepdims=True),
                    (8, embed.shape[1]),
                ),
            ],
            axis=0,
        )
        gram[...] = lax.dot_general(
            centred, centred, (((1,), (1,)), ((), ())),
            precision=lax.Precision.HIGHEST, preferred_element_type=F32,
        ) * (1.0 / embed.shape[1])
        high, low = two_parts(gram[:lat, :lat])
        gram_split[:lat] = high
        gram_split[lat:] = low
        turned[width_q : width_q + lat, :lat] = high
        turned[width_q : width_q + lat, lat:] = low
        across = lax.broadcasted_iota(jnp.int32, (lat, 2 * lat), 1)
        down = lax.broadcasted_iota(jnp.int32, (lat, 2 * lat), 0)
        turned[width_q + lat :] = (across == down).astype(BF16)
        gained[...] = jnp.concatenate(two_parts(centred * norm_gain[...]), axis=0)

    def merge(which):
        loads[1 + which].wait()
        product = dot(gained[...], w_joined[which])
        product = product[: lat + 8] + product[lat + 8 :]
        if which == 0:
            product = product * (HEAD_DIM**-0.5 * math.log2(math.e))
            high, low = two_parts(product[:lat].T)
            turned_query[:, :lat] = high
            turned_query[:, lat:] = low
            query_lift[...] = product[lat:].T
        elif which == 1:
            high, low = two_parts(product[:lat])
            split_key[:lat] = high
            split_key[lat:] = low
            key_offset[...] = product[lat:]
        else:
            high, low = two_parts(product[:lat].T)
            turned[:width_q, :lat] = high
            turned[:width_q, lat:] = low
            lift[...] = product[lat:].T

    kernels[0][1].wait()
    keep(0)
    merge_gram()
    merge(2)
    take_time(0, middle)
    first = activate(0, middle, bias_one[...]).astype(BF16)
    field[1, 1, 2:rows] = first.reshape(-1, width, chans)
    shift(1, 2, rows - 2)
    take_time(0, edges)
    first = activate(0, edges, bias_one[...]).astype(BF16)
    field[1, 1, 1] = first[:width]
    field[1, 1, rows] = first[width:]
    send_rows(1)
    shift(1, 1, 1)
    shift(1, rows, 1)
    for at in (0, 2, 1):
        kernels[1][at].wait()
    send_time(1, middle)
    merge(1)
    take_rows(1)
    send_time(1, edges)
    keep(1)
    merge(0)
    for one in small[4:]:
        one.wait()

    def finish(part):
        here = field[1, 1, 2:rows] if part == middle else jnp.concatenate(
            [field[1, 1, 1], field[1, 1, rows]], axis=0
        )
        own = here.reshape(-1, chans).astype(F32)
        return (own + activate(1, part, bias_two[...])).astype(BF16)

    take_time(1, middle)
    inner = finish(middle)
    take_time(1, edges)
    outer = finish(edges)
    lines = [outer[:width]]
    lines += [inner[at * width : (at + 1) * width] for at in range(rows - 2)]
    lines += [outer[width:]]

    line = width // 2
    for block in range(rows // 2):
        for col in range(2):
            pair[col] = dot(lines[2 * block], patch_weight[0, col]) + dot(
                lines[2 * block + 1], patch_weight[1, col]
            )
        patches = (
            pair[0, pl.ds(0, line, stride=2), :] + pair[1, pl.ds(1, line, stride=2), :]
            + patch_bias[...]
        ).astype(BF16)
        gathered[aa, ba, pl.ds(block * line, line), :] = patches

    for head in range(heads):
        slot = slice((1 - head % 2) * HEAD_DIM, (2 - head % 2) * HEAD_DIM)
        queries[head, slot] = jnp.zeros((HEAD_DIM, queries.shape[2]), BF16)
    values[:, HEAD_DIM:] = jnp.ones((heads, values.shape[1] - HEAD_DIM, values.shape[2]), BF16)

    flanked = jnp.minimum(aa, n_aa - 1 - aa)
    toward = jnp.where(aa < n_aa - 1 - aa, 1, -1)

    def frame_of(step):
        near = (1 - 2 * ((step + 1) % 2)) * ((step + 1) // 2)
        return aa + jnp.where(step <= 2 * flanked, near, toward * (step - flanked))

    def piece(frame, block, send_sem, to_aa, to_ba):
        here = gathered.at[frame, block]
        return pltpu.make_async_remote_copy(
            src_ref=here, dst_ref=here, send_sem=send_sem, recv_sem=token_recv.at[frame, block],
            device_id=(to_aa, to_ba), device_id_type=MESH,
        )

    def along_aa(step):
        return piece(aa, ba, aa_send.at[step], frame_of(step), ba)

    def along_ba(step, hop):
        return piece(frame_of(step), ba, ba_send.at[step, hop], aa, (ba + 2 * hop) % n_ba)

    def to_partner(step, hop):
        block = (ba + n_ba - 2 * hop) % n_ba
        return piece(frame_of(step), block, core_send.at[step, hop], aa, partner)

    def landed(frame, block):
        piece(frame, block, aa_send.at[0], aa, partner).wait_recv()

    slope = 2.0 * gram[lat : lat + 1, :lat]
    slope_down = 2.0 * gram[:lat, lat : lat + 1]
    floor = gram[lat : lat + 1, lat : lat + 1]

    def take_pairs(step, hops, with_queries):
        frame = frame_of(step)
        blocks = [((ba + n_ba - 2 * hop) % n_ba) // 2 for hop in hops]
        size = 2 * tokens
        latents = jnp.concatenate(
            [gathered[frame, pl.ds(2 * block, 2)].reshape(size, lat) for block in blocks], axis=0
        )
        twice = jnp.concatenate([latents, latents], axis=1)
        bent = dot(twice, gram_split[...]) + slope
        power = (bent * latents.astype(F32)).sum(-1, keepdims=True) + floor
        scale = lax.rsqrt(jnp.maximum(power, 0.0) + 1e-05)
        projected = ((dot(twice, split_key[...]) + key_offset[:1]) * scale).astype(BF16)
        down = lax.dot_general(
            turned[...], twice, (((1,), (1,)), ((), ())), preferred_element_type=F32
        )
        bent = (down[width_q : width_q + lat] + slope_down) * down[width_q + lat :]
        power = bent.sum(0, keepdims=True) + floor
        scale_down = lax.rsqrt(jnp.maximum(power, 0.0) + 1e-05)
        flipped = ((down[:width_q] + lift[:, :1]) * scale_down).astype(BF16)
        for index, block in enumerate(blocks):
            own = slice(index * size, (index + 1) * size)
            at = pl.ds(pl.multiple_of((frame * half + block) * size, size), size)
            for couple in range(heads // 2):
                keys[couple, at] = projected[own, couple * SLOT : (couple + 1) * SLOT]
            for head in range(heads):
                values[head, :HEAD_DIM, at] = flipped[head * HEAD_DIM : (head + 1) * HEAD_DIM, own]
        if with_queries:
            down = lax.dot_general(
                turned_query[...], twice, (((1,), (1,)), ((), ())), preferred_element_type=F32
            )
            asked = ((down + query_lift[:, :1]) * scale_down).astype(BF16)
            for index, block in enumerate(blocks):
                own = slice(index * size, (index + 1) * size)
                there = pl.ds(pl.multiple_of(block * size, size), size)
                for head in range(heads):
                    slot = slice(head % 2 * HEAD_DIM, (head % 2 + 1) * HEAD_DIM)
                    queries[head, slot, there] = asked[head * HEAD_DIM : (head + 1) * HEAD_DIM, own]

    def pass_on(step):
        for hop in range(1, half):
            along_ba(step, hop).start()
        to_partner(step, 0).start()

    def advance(step):
        landed(frame_of(step), ba)
        pass_on(step)

    def hand_over(step):
        @pl.loop(1, half)
        def _(hop):
            landed(frame_of(step), (ba + n_ba - 2 * hop) % n_ba)
            to_partner(step, hop).start()

    def take(step, hop, with_queries):
        landed(frame_of(step), (partner + n_ba - 2 * hop) % n_ba)
        take_pairs(step, [hop], with_queries)

    def take_rest(step, with_queries):
        @pl.loop(1, half)
        def _(hop):
            take(step, hop, with_queries)

    for step in range(1, n_aa):
        along_aa(step).start()
    pass_on(0)
    sent(0)
    sent(1)
    take(0, 0, True)
    advance(1)
    hand_over(0)

    @pl.loop(1, half)
    def _(hop):
        take(0, hop, True)
        pl.when(hop + 1 < n_aa)(lambda: advance(hop + 1))

    for step in range(half + 1, n_aa):
        advance(step)
    hand_over(1)
    take(1, 0, False)

    @pl.loop(2, n_aa)
    def _(step):
        hand_over(step)
        take_rest(step - 1, False)
        take(step, 0, False)

    take_rest(n_aa - 1, False)

    for step in range(1, n_aa):
        along_aa(step).wait_send()

    @pl.loop(0, n_aa)
    def _(step):
        to_partner(step, 0).wait_send()

        @pl.loop(1, half)
        def _(hop):
            along_ba(step, hop).wait_send()
            to_partner(step, hop).wait_send()

    def share(dest):
        offset = (dest + n_ba - ba) % n_ba
        return pltpu.make_async_remote_copy(
            src_ref=shares.at[dest], dst_ref=arrived.at[ba],
            send_sem=share_send.at[offset], recv_sem=share_recv.at[offset],
            device_id=(aa, dest), device_id_type=MESH,
        )

    total = keys.shape[1]
    big = math.gcd(total, 4096)

    def attend(at):
        per_span = span // tokens
        where = pl.ds(pl.multiple_of(at * span, span), span)

        def sweep(group, asked, base, state):
            order = [(each, part) for each in range(len(asked)) for part in range(big // chunk)]

            def held(part):
                return pl.ds(pl.multiple_of(base + part * chunk, chunk), chunk)

            def score(each, part):
                return dot(keys[(group + each) // 2, held(part)], asked[each])

            def gather(each, part, shrink, probs):
                best, accum = state[each]
                added = dot(values[group + each, :, held(part)], probs)
                return added if shrink is None else accum * shrink + added

            ahead = [score(*one) for one in order[:LOOK]]
            late = None
            for index, (each, part) in enumerate(order):
                if index + LOOK < len(order):
                    ahead.append(score(*order[index + LOOK]))
                scores, ahead[index] = ahead[index], None
                best, accum = state[each]
                peak = scores.max(0, keepdims=True)
                shrink = None
                if best is not None:
                    peak = jnp.maximum(best, peak)
                    shrink = jnp.exp2(best - peak)
                probs = jnp.exp2(scores - peak).astype(BF16)
                if late is not None:
                    state[late[0]] = (state[late[0]][0], gather(*late))
                state[each] = (peak, state[each][1])
                late = (each, part, shrink, probs)
            state[late[0]] = (state[late[0]][0], gather(*late))
            return state

        @pl.loop(0, heads // group_size)
        def _(index):
            group = index * group_size
            asked = [queries[group + each, :, where] for each in range(group_size)]
            if total == big:
                state = sweep(group, asked, 0, [(None, None)] * group_size)
            else:
                empty = (jnp.full((1, span), -jnp.inf, F32), jnp.zeros((values.shape[1], span), F32))

                def one_big(index, state):
                    return tuple(sweep(group, asked, index * big, list(state)))

                state = lax.fori_loop(0, total // big, one_big, (empty,) * group_size)
            for each in range(group_size):
                accum = state[each][1]
                rows = pl.ds(pl.multiple_of((group + each) * HEAD_DIM, HEAD_DIM), HEAD_DIM)
                attended[rows] = (accum[:HEAD_DIM] / accum[HEAD_DIM : HEAD_DIM + 1]).astype(BF16)

        velocity = lax.dot_general(
            w_velocity[...], attended[...], (((0,), (0,)), ((), ())), preferred_element_type=F32
        )
        for part in range(per_span):
            dest = at * per_span + part
            shares[dest] = velocity[:, part * tokens : (part + 1) * tokens].astype(BF16)

            @pl.when(dest != ba)
            def _():
                share(dest).start()

    spans = n_ba * tokens // span

    @pl.loop(1, spans + 1)
    def _(step):
        attend((ba * tokens // span + step) % spans)

    summed = shares[ba].astype(F32)
    for offset in range(1, n_ba):
        share((ba + offset) % n_ba).wait_recv()
        summed += arrived[(ba + n_ba - offset) % n_ba].astype(F32)
    out[...] = summed.T
    for offset in range(1, n_ba):
        share((ba + offset) % n_ba).wait_send()


def on_device(
    n_aa, n_ba,
    feats, conv_one, bias_one, conv_two, bias_two, patch_weight, patch_bias,
    embed_weight, embed_bias, norm_gain, w_query, w_key, w_value, w_velocity,
):
    _, rows, width, chans = feats.shape
    lat = patch_bias.shape[0]
    features, qwidth = w_query.shape
    heads = qwidth // HEAD_DIM
    tokens = rows * width // 4
    total = n_ba * n_aa * tokens
    span = max(tokens, min(512, n_ba * tokens))
    chunk = math.gcd(total, 256)
    vmem = pl.BlockSpec(memory_space=pltpu.VMEM)
    anywhere = pl.BlockSpec(memory_space=pl.ANY)
    dma = pltpu.SemaphoreType.DMA
    return pl.pallas_call(
        functools.partial(whole_kernel, n_aa, n_ba, span, chunk),
        out_shape=jax.ShapeDtypeStruct((tokens, lat), F32),
        in_specs=[anywhere] * 14,
        out_specs=vmem,
        scratch_shapes=[
            pltpu.VMEM((1, chans), F32),
            pltpu.VMEM((1, chans), F32),
            pltpu.VMEM((2, 2, chans, lat), BF16),
            pltpu.VMEM((1, lat), F32),
            pltpu.VMEM((lat, features), BF16),
            pltpu.VMEM((1, features), F32),
            pltpu.VMEM((1, features), F32),
            pltpu.VMEM((qwidth, lat), BF16),
            pltpu.VMEM((2 * lat + 16, features), BF16),
            pltpu.VMEM((2, 3, rows + 2, width, chans), BF16),
            pltpu.VMEM((2, 9, chans, 3 * chans), BF16),
            pltpu.VMEM((3, features, qwidth), BF16),
            pltpu.VMEM((2, 2, rows, width, chans), BF16),
            pltpu.VMEM((2, 2, rows, width, chans), BF16),
            pltpu.VMEM((rows, width, chans), F32),
            pltpu.VMEM((2, width, lat), F32),
            pltpu.VMEM((n_aa, n_ba, tokens, lat), BF16),
            pltpu.VMEM((qwidth, 2 * lat), BF16),
            pltpu.VMEM((qwidth, 8), F32),
            pltpu.VMEM((2 * lat, qwidth), BF16),
            pltpu.VMEM((8, qwidth), F32),
            pltpu.VMEM((qwidth + 2 * lat, 2 * lat), BF16),
            pltpu.VMEM((qwidth, 8), F32),
            pltpu.VMEM((2 * lat, lat), BF16),
            pltpu.VMEM((lat + 8, lat + 8), F32),
            pltpu.VMEM((heads, SLOT, n_ba * tokens), BF16),
            pltpu.VMEM((heads // 2, total, SLOT), BF16),
            pltpu.VMEM((heads, STACK, total), BF16),
            pltpu.VMEM((qwidth, span), BF16),
            pltpu.VMEM((n_ba, lat, tokens), BF16),
            pltpu.VMEM((n_ba, lat, tokens), BF16),
            dma((10,)), dma((8,)),
            dma((2, 2, 2)), dma((2, 2, 2)), dma((2, 2)), dma((2, 2)),
            dma((n_aa, n_ba)), dma((n_aa,)), dma((n_aa, n_ba // 2)), dma((n_aa, n_ba // 2)),
            dma((n_ba,)), dma((n_ba,)),
        ],
        compiler_params=pltpu.CompilerParams(
            collective_id=0, has_side_effects=True, vmem_limit_bytes=VMEM_BYTES
        ),
        name="whole",
    )(
        feats, conv_one.reshape(3, 9, chans, chans), bias_one[None],
        conv_two.reshape(3, 9, chans, chans), bias_two[None],
        patch_weight, patch_bias[None], embed_weight, embed_bias[None], norm_gain[None],
        w_query, w_key, w_value, w_velocity,
    )


def solution(mesh):
    return jax.shard_map(
        functools.partial(on_device, mesh.shape["aa"], mesh.shape["ba"]),
        mesh=mesh,
        in_specs=(
            P("aa", "ba", None, None), P(), P(), P(), P(), P(), P(), P(), P(), P(),
            P(None, "ba"), P(None, "ba"), P(None, "ba"), P("ba", None),
        ),
        out_specs=P(("aa", "ba"), None),
        check_vma=False,
    )
```

```python
import functools
import math

import jax
import jax.numpy as jnp
from jax import lax
from jax.experimental import pallas as pl
from jax.experimental.pallas import tpu as pltpu
from jax.sharding import PartitionSpec as P

HEAD_DIM = 64
SLOT = 128
MESH = pl.DeviceIdType.MESH
LOOK = 1
GROUPED = 4
STACK = HEAD_DIM + 16
F32 = jnp.float32
BF16 = jnp.bfloat16
VMEM_BYTES = 67043328


def dot(left, right):
    return jnp.dot(left, right, preferred_element_type=F32)


def two_parts(value):
    high = value.astype(BF16)
    return high, (value - high.astype(F32)).astype(BF16)


def gelu(value):
    return 0.5 * value * (1.0 + lax.erf(value * (0.5**0.5)))


def whole_kernel(
    n_aa, n_ba, span, chunk,
    feats, conv_one, bias_one_in, conv_two, bias_two_in, patch_weight_in, patch_bias_in,
    embed_weight_in, embed_bias_in, norm_gain_in, w_query, w_key, w_value, w_velocity_in,
    out,
    bias_one, bias_two, patch_weight, patch_bias, embed_weight, embed_bias, norm_gain, w_velocity, gained,
    field, taps, w_joined, outgoing, incoming, acc, pair, gathered, turned_query, query_lift, split_key, key_offset, turned, lift,
    gram_split, gram, queries, keys, values, attended, shares, arrived,
    load_sem, small_sem, aa_side_send, aa_side_recv, ba_side_send, ba_side_recv,
    token_recv, aa_send, ba_send, core_send, share_send, share_recv,
):
    aa, ba = lax.axis_index("aa"), lax.axis_index("ba")
    _, rows, width, chans = feats.shape
    partner = ba + 1 - 2 * (ba % 2)
    half = n_ba // 2
    width_q = w_query.shape[1]
    heads = width_q // HEAD_DIM
    group_size = math.gcd(heads, GROUPED)
    tokens = rows * width // 4
    lat = patch_bias.shape[1]

    def load(source, target, at):
        return pltpu.make_async_copy(source, target, load_sem.at[at])

    loads = [
        load(feats.at[0], field.at[0, 1, pl.ds(1, rows)], 0),
        load(w_query, w_joined.at[0], 1),
        load(w_key, w_joined.at[1], 2),
        load(w_value, w_joined.at[2], 3),
    ]
    kernels = [
        [load(source.at[at], taps.at[which, :, :, pl.ds(column * chans, chans)], 4 + 3 * which + at)
         for at, column in enumerate((0, 2, 1))]
        for which, source in enumerate((conv_one, conv_two))
    ]
    small = [
        pltpu.make_async_copy(source, target, small_sem.at[at])
        for at, (source, target) in enumerate((
            (bias_one_in, bias_one), (embed_weight_in, embed_weight), (embed_bias_in, embed_bias),
            (norm_gain_in, norm_gain), (bias_two_in, bias_two), (patch_weight_in, patch_weight),
            (patch_bias_in, patch_bias), (w_velocity_in, w_velocity),
        ))
    ]
    loads[0].start()
    for at in (0, 2, 1):
        kernels[0][at].start()
    for one in small[:4]:
        one.start()
    for one in loads[1:]:
        one.start()
    for at in (0, 2, 1):
        kernels[1][at].start()
    for one in small[4:]:
        one.start()

    def aa_there(side):
        return aa > 0 if side == -1 else aa < n_aa - 1

    def ba_there(side):
        return ba > 0 if side == -1 else ba < n_ba - 1

    barrier = pltpu.get_barrier_semaphore()
    for step in range(1, n_aa):
        pl.semaphore_signal(
            barrier, inc=1, device_id=((aa + step) % n_aa, ba), device_id_type=MESH
        )
    for step in range(1, n_ba):
        pl.semaphore_signal(
            barrier, inc=1, device_id=(aa, (ba + step) % n_ba), device_id_type=MESH
        )

    edges, middle, both = 0, 1, 2
    parts = (slice(0, 2), slice(2, rows))

    def along_time(which, side, part):
        at = (which, (side + 1) // 2, part)
        here = (which, (side + 1) // 2, parts[part])
        return pltpu.make_async_remote_copy(
            src_ref=outgoing.at[here], dst_ref=incoming.at[here],
            send_sem=aa_side_send.at[at], recv_sem=aa_side_recv.at[at],
            device_id=(aa + side, ba), device_id_type=MESH,
        )

    def along_rows(which, side):
        source, target = (rows, 0) if side == 1 else (1, rows + 1)
        at = (which, (side + 1) // 2)
        return pltpu.make_async_remote_copy(
            src_ref=field.at[which, 1, source], dst_ref=field.at[which, 1, target],
            send_sem=ba_side_send.at[at], recv_sem=ba_side_recv.at[at],
            device_id=(aa, ba + side), device_id_type=MESH,
        )

    def send_rows(which):
        for side in (-1, 1):
            pl.when(ba_there(side))(along_rows(which, side).start)

    def take_rows(which):
        for side in (-1, 1):
            pl.when(ba_there(-side))(along_rows(which, side).wait_recv)
        shift(which, 0, 1)
        shift(which, rows + 1, 1)

    def take_time(which, part):
        for side in (-1, 1):
            pl.when(aa_there(-side))(along_time(which, side, part).wait_recv)

    def sent(which):
        for side in (-1, 1):
            pl.when(ba_there(side))(along_rows(which, side).wait_send)
            for part in (edges, middle):
                pl.when(aa_there(side))(along_time(which, side, part).wait_send)

    def blank():
        line = jnp.zeros((width, chans), BF16)
        for which in range(2):
            for side, row in ((-1, 0), (1, rows + 1)):
                @pl.when(jnp.logical_not(ba_there(side)))
                def _():
                    field[which, 1, row] = line

                @pl.when(jnp.logical_not(aa_there(side)))
                def _():
                    for at in range(rows):
                        incoming[which, (1 - side) // 2, at] = line

    def shift(which, row, count):
        here = pl.ds(row, count)
        held = field[which, 1, here].reshape(count * width, chans).astype(F32)
        place = lax.broadcasted_iota(jnp.int32, held.shape, 0) % width
        before = jnp.where(place == 0, 0.0, pltpu.roll(held, 1, 0))
        after = jnp.where(place == width - 1, 0.0, pltpu.roll(held, count * width - 1, 0))
        field[which, 0, here] = before.astype(BF16).reshape(count, width, chans)
        field[which, 2, here] = after.astype(BF16).reshape(count, width, chans)

    def stack(which, part):
        def window(shift_r, shift_w):
            if part == middle:
                held = field[which, shift_w, pl.ds(1 + shift_r, rows - 2)]
                return held.reshape((rows - 2) * width, chans)
            if part == both:
                return field[which, shift_w, pl.ds(shift_r, rows)].reshape(rows * width, chans)
            return jnp.concatenate(
                [field[which, shift_w, shift_r], field[which, shift_w, rows - 1 + shift_r]], axis=0
            )

        return jnp.concatenate(
            [window(shift_r, shift_w) for shift_r in range(3) for shift_w in range(3)], axis=1
        )

    def send_time(which, part):
        made = dot(
            stack(which, part), taps[which, :, :, : 2 * chans].reshape(9 * chans, 2 * chans)
        ).astype(BF16)
        for side, column in ((-1, chans), (1, 0)):
            outgoing[which, (side + 1) // 2, parts[part]] = made[
                :, column : column + chans
            ].reshape(-1, width, chans)
            pl.when(aa_there(side))(along_time(which, side, part).start)

    def keep(which):
        acc[...] = dot(
            stack(which, both), taps[which, :, :, 2 * chans :].reshape(9 * chans, chans)
        ).reshape(rows, width, chans)

    def activate(which, part, bias):
        here = parts[part]
        kept = acc[1 : rows - 1] if part == middle else jnp.concatenate(
            [acc[:1], acc[rows - 1 :]], axis=0
        )
        total = kept + incoming[which, 0, here].astype(F32)
        total += incoming[which, 1, here].astype(F32)
        return gelu(total.reshape(-1, chans) + bias)

    blank()
    loads[0].wait()
    shift(0, 1, rows)
    pl.semaphore_wait(barrier, n_aa - 1 + n_ba - 1)
    send_rows(0)
    kernels[0][0].wait()
    kernels[0][2].wait()
    send_time(0, middle)
    take_rows(0)
    send_time(0, edges)

    def merge_gram():
        for one in small[:4]:
            one.wait()
        embed = embed_weight[...].astype(F32)
        centred = jnp.concatenate(
            [
                embed - embed.mean(-1, keepdims=True),
                jnp.broadcast_to(
                    embed_bias[...] - embed_bias[...].mean(-1, keepdims=True),
                    (8, embed.shape[1]),
                ),
            ],
            axis=0,
        )
        gram[...] = lax.dot_general(
            centred, centred, (((1,), (1,)), ((), ())),
            precision=lax.Precision.HIGHEST, preferred_element_type=F32,
        ) * (1.0 / embed.shape[1])
        high, low = two_parts(gram[:lat, :lat])
        gram_split[:lat] = high
        gram_split[lat:] = low
        turned[width_q : width_q + lat, :lat] = high
        turned[width_q : width_q + lat, lat:] = low
        across = lax.broadcasted_iota(jnp.int32, (lat, 2 * lat), 1)
        down = lax.broadcasted_iota(jnp.int32, (lat, 2 * lat), 0)
        turned[width_q + lat :] = (across == down).astype(BF16)
        gained[...] = jnp.concatenate(two_parts(centred * norm_gain[...]), axis=0)

    def merge(which):
        loads[1 + which].wait()
        product = dot(gained[...], w_joined[which])
        product = product[: lat + 8] + product[lat + 8 :]
        if which == 0:
            product = product * (HEAD_DIM**-0.5 * math.log2(math.e))
            high, low = two_parts(product[:lat].T)
            turned_query[:, :lat] = high
            turned_query[:, lat:] = low
            query_lift[...] = product[lat:].T
        elif which == 1:
            high, low = two_parts(product[:lat])
            split_key[:lat] = high
            split_key[lat:] = low
            key_offset[...] = product[lat:]
        else:
            high, low = two_parts(product[:lat].T)
            turned[:width_q, :lat] = high
            turned[:width_q, lat:] = low
            lift[...] = product[lat:].T

    kernels[0][1].wait()
    keep(0)
    merge_gram()
    merge(2)
    take_time(0, middle)
    first = activate(0, middle, bias_one[...]).astype(BF16)
    field[1, 1, 2:rows] = first.reshape(-1, width, chans)
    shift(1, 2, rows - 2)
    take_time(0, edges)
    first = activate(0, edges, bias_one[...]).astype(BF16)
    field[1, 1, 1] = first[:width]
    field[1, 1, rows] = first[width:]
    send_rows(1)
    shift(1, 1, 1)
    shift(1, rows, 1)
    for at in (0, 2, 1):
        kernels[1][at].wait()
    send_time(1, middle)
    merge(1)
    take_rows(1)
    send_time(1, edges)
    keep(1)
    merge(0)
    for one in small[4:]:
        one.wait()

    def finish(part):
        here = field[1, 1, 2:rows] if part == middle else jnp.concatenate(
            [field[1, 1, 1], field[1, 1, rows]], axis=0
        )
        own = here.reshape(-1, chans).astype(F32)
        return (own + activate(1, part, bias_two[...])).astype(BF16)

    take_time(1, middle)
    inner = finish(middle)
    take_time(1, edges)
    outer = finish(edges)
    lines = [outer[:width]]
    lines += [inner[at * width : (at + 1) * width] for at in range(rows - 2)]
    lines += [outer[width:]]

    stacked = jnp.concatenate(
        [jnp.concatenate(lines[2 * block : 2 * block + 2], axis=1) for block in range(rows // 2)],
        axis=0,
    )
    square = jnp.concatenate(
        [jnp.concatenate([patch_weight[row, col] for col in range(2)], axis=1) for row in range(2)],
        axis=0,
    )
    both_columns = dot(stacked, square)
    for col in range(2):
        pair[col] = both_columns[:, col * lat : (col + 1) * lat]
    patches = (
        pair[0, pl.ds(0, tokens, stride=2), :] + pair[1, pl.ds(1, tokens, stride=2), :]
        + patch_bias[...]
    ).astype(BF16)
    gathered[aa, ba] = patches

    for head in range(heads):
        slot = slice((1 - head % 2) * HEAD_DIM, (2 - head % 2) * HEAD_DIM)
        queries[head, slot] = jnp.zeros((HEAD_DIM, queries.shape[2]), BF16)
    values[:, HEAD_DIM:] = jnp.ones((heads, values.shape[1] - HEAD_DIM, values.shape[2]), BF16)

    flanked = jnp.minimum(aa, n_aa - 1 - aa)
    toward = jnp.where(aa < n_aa - 1 - aa, 1, -1)

    def frame_of(step):
        near = (1 - 2 * ((step + 1) % 2)) * ((step + 1) // 2)
        return aa + jnp.where(step <= 2 * flanked, near, toward * (step - flanked))

    def piece(frame, block, send_sem, to_aa, to_ba):
        here = gathered.at[frame, block]
        return pltpu.make_async_remote_copy(
            src_ref=here, dst_ref=here, send_sem=send_sem, recv_sem=token_recv.at[frame, block],
            device_id=(to_aa, to_ba), device_id_type=MESH,
        )

    def along_aa(step):
        return piece(aa, ba, aa_send.at[step], frame_of(step), ba)

    def along_ba(step, hop):
        return piece(frame_of(step), ba, ba_send.at[step, hop], aa, (ba + 2 * hop) % n_ba)

    def to_partner(step, hop):
        block = (ba + n_ba - 2 * hop) % n_ba
        return piece(frame_of(step), block, core_send.at[step, hop], aa, partner)

    def landed(frame, block):
        piece(frame, block, aa_send.at[0], aa, partner).wait_recv()

    slope = 2.0 * gram[lat : lat + 1, :lat]
    slope_down = 2.0 * gram[:lat, lat : lat + 1]
    floor = gram[lat : lat + 1, lat : lat + 1]

    def take_pairs(step, hops, with_queries):
        frame = frame_of(step)
        blocks = [((ba + n_ba - 2 * hop) % n_ba) // 2 for hop in hops]
        size = 2 * tokens
        latents = jnp.concatenate(
            [gathered[frame, pl.ds(2 * block, 2)].reshape(size, lat) for block in blocks], axis=0
        )
        twice = jnp.concatenate([latents, latents], axis=1)
        bent = dot(twice, gram_split[...]) + slope
        power = (bent * latents.astype(F32)).sum(-1, keepdims=True) + floor
        scale = lax.rsqrt(jnp.maximum(power, 0.0) + 1e-05)
        projected = ((dot(twice, split_key[...]) + key_offset[:1]) * scale).astype(BF16)
        down = lax.dot_general(
            turned[...], twice, (((1,), (1,)), ((), ())), preferred_element_type=F32
        )
        bent = (down[width_q : width_q + lat] + slope_down) * down[width_q + lat :]
        power = bent.sum(0, keepdims=True) + floor
        scale_down = lax.rsqrt(jnp.maximum(power, 0.0) + 1e-05)
        flipped = ((down[:width_q] + lift[:, :1]) * scale_down).astype(BF16)
        for index, block in enumerate(blocks):
            own = slice(index * size, (index + 1) * size)
            at = pl.ds(pl.multiple_of((frame * half + block) * size, size), size)
            for couple in range(heads // 2):
                keys[couple, at] = projected[own, couple * SLOT : (couple + 1) * SLOT]
            for head in range(heads):
                values[head, :HEAD_DIM, at] = flipped[head * HEAD_DIM : (head + 1) * HEAD_DIM, own]
        if with_queries:
            down = lax.dot_general(
                turned_query[...], twice, (((1,), (1,)), ((), ())), preferred_element_type=F32
            )
            asked = ((down + query_lift[:, :1]) * scale_down).astype(BF16)
            for index, block in enumerate(blocks):
                own = slice(index * size, (index + 1) * size)
                there = pl.ds(pl.multiple_of(block * size, size), size)
                for head in range(heads):
                    slot = slice(head % 2 * HEAD_DIM, (head % 2 + 1) * HEAD_DIM)
                    queries[head, slot, there] = asked[head * HEAD_DIM : (head + 1) * HEAD_DIM, own]

    def pass_on(step):
        for hop in range(1, half):
            along_ba(step, hop).start()
        to_partner(step, 0).start()

    def advance(step):
        landed(frame_of(step), ba)
        pass_on(step)

    def hand_over(step):
        @pl.loop(1, half)
        def _(hop):
            landed(frame_of(step), (ba + n_ba - 2 * hop) % n_ba)
            to_partner(step, hop).start()

    def take(step, hop, with_queries):
        landed(frame_of(step), (partner + n_ba - 2 * hop) % n_ba)
        take_pairs(step, [hop], with_queries)

    def take_all(pairs, with_queries):
        for step, hop in pairs:
            landed(frame_of(step), (partner + n_ba - 2 * hop) % n_ba)
        for step, hop in pairs:
            take_pairs(step, [hop], with_queries)

    def take_rest(step, also, with_queries):
        batch = max(each for each in (1, 2, 3) if (half - 1) % each == 0)

        @pl.loop(0, (half - 1) // batch - 1)
        def _(index):
            take_all([(step, 1 + index * batch + each) for each in range(batch)], with_queries)

        take_all([(step, half - 1 - each) for each in range(batch)] + also, with_queries)

    for step in range(1, n_aa):
        along_aa(step).start()
    pass_on(0)
    sent(0)
    sent(1)
    take(0, 0, True)
    advance(1)
    hand_over(0)

    @pl.loop(1, half)
    def _(hop):
        take(0, hop, True)
        pl.when(hop + 1 < n_aa)(lambda: advance(hop + 1))

    for step in range(half + 1, n_aa):
        advance(step)
    hand_over(1)
    take(1, 0, False)

    @pl.loop(2, n_aa)
    def _(step):
        hand_over(step)
        take_rest(step - 1, [(step, 0)], False)

    take_rest(n_aa - 1, [], False)

    for step in range(1, n_aa):
        along_aa(step).wait_send()

    @pl.loop(0, n_aa)
    def _(step):
        to_partner(step, 0).wait_send()

        @pl.loop(1, half)
        def _(hop):
            along_ba(step, hop).wait_send()
            to_partner(step, hop).wait_send()

    def share(dest):
        offset = (dest + n_ba - ba) % n_ba
        return pltpu.make_async_remote_copy(
            src_ref=shares.at[dest], dst_ref=arrived.at[ba],
            send_sem=share_send.at[offset], recv_sem=share_recv.at[offset],
            device_id=(aa, dest), device_id_type=MESH,
        )

    total = keys.shape[1]
    big = math.gcd(total, 4096)

    def attend(at):
        per_span = span // tokens
        where = pl.ds(pl.multiple_of(at * span, span), span)

        def sweep(group, asked, base, state):
            order = [(each, part) for each in range(len(asked)) for part in range(big // chunk)]

            def held(part):
                return pl.ds(pl.multiple_of(base + part * chunk, chunk), chunk)

            def score(each, part):
                return dot(keys[(group + each) // 2, held(part)], asked[each])

            def gather(each, part, shrink, probs):
                best, accum = state[each]
                added = dot(values[group + each, :, held(part)], probs)
                return added if shrink is None else accum * shrink + added

            ahead = [score(*one) for one in order[:LOOK]]
            late = None
            for index, (each, part) in enumerate(order):
                if index + LOOK < len(order):
                    ahead.append(score(*order[index + LOOK]))
                scores, ahead[index] = ahead[index], None
                best, accum = state[each]
                peak = scores.max(0, keepdims=True)
                shrink = None
                if best is not None:
                    peak = jnp.maximum(best, peak)
                    shrink = jnp.exp2(best - peak)
                probs = jnp.exp2(scores - peak).astype(BF16)
                if late is not None:
                    state[late[0]] = (state[late[0]][0], gather(*late))
                state[each] = (peak, state[each][1])
                late = (each, part, shrink, probs)
            state[late[0]] = (state[late[0]][0], gather(*late))
            return state

        @pl.loop(0, heads // group_size)
        def _(index):
            group = index * group_size
            asked = [queries[group + each, :, where] for each in range(group_size)]
            if total == big:
                state = sweep(group, asked, 0, [(None, None)] * group_size)
            else:
                empty = (jnp.full((1, span), -jnp.inf, F32), jnp.zeros((values.shape[1], span), F32))

                def one_big(index, state):
                    return tuple(sweep(group, asked, index * big, list(state)))

                state = lax.fori_loop(0, total // big, one_big, (empty,) * group_size)
            for each in range(group_size):
                accum = state[each][1]
                rows = pl.ds(pl.multiple_of((group + each) * HEAD_DIM, HEAD_DIM), HEAD_DIM)
                attended[rows] = (accum[:HEAD_DIM] / accum[HEAD_DIM : HEAD_DIM + 1]).astype(BF16)

        velocity = lax.dot_general(
            w_velocity[...], attended[...], (((0,), (0,)), ((), ())), preferred_element_type=F32
        )
        for part in range(per_span):
            dest = at * per_span + part
            shares[dest] = velocity[:, part * tokens : (part + 1) * tokens].astype(BF16)

            @pl.when(dest != ba)
            def _():
                share(dest).start()

    spans = n_ba * tokens // span

    @pl.loop(1, spans + 1)
    def _(step):
        attend((ba * tokens // span + step) % spans)

    summed = shares[ba].astype(F32)
    for offset in range(1, n_ba):
        share((ba + offset) % n_ba).wait_recv()
        summed += arrived[(ba + n_ba - offset) % n_ba].astype(F32)
    out[...] = summed.T
    for offset in range(1, n_ba):
        share((ba + offset) % n_ba).wait_send()


def on_device(
    n_aa, n_ba,
    feats, conv_one, bias_one, conv_two, bias_two, patch_weight, patch_bias,
    embed_weight, embed_bias, norm_gain, w_query, w_key, w_value, w_velocity,
):
    _, rows, width, chans = feats.shape
    lat = patch_bias.shape[0]
    features, qwidth = w_query.shape
    heads = qwidth // HEAD_DIM
    tokens = rows * width // 4
    total = n_ba * n_aa * tokens
    span = max(tokens, min(512, n_ba * tokens))
    chunk = math.gcd(total, 256)
    vmem = pl.BlockSpec(memory_space=pltpu.VMEM)
    anywhere = pl.BlockSpec(memory_space=pl.ANY)
    dma = pltpu.SemaphoreType.DMA
    return pl.pallas_call(
        functools.partial(whole_kernel, n_aa, n_ba, span, chunk),
        out_shape=jax.ShapeDtypeStruct((tokens, lat), F32),
        in_specs=[anywhere] * 14,
        out_specs=vmem,
        scratch_shapes=[
            pltpu.VMEM((1, chans), F32),
            pltpu.VMEM((1, chans), F32),
            pltpu.VMEM((2, 2, chans, lat), BF16),
            pltpu.VMEM((1, lat), F32),
            pltpu.VMEM((lat, features), BF16),
            pltpu.VMEM((1, features), F32),
            pltpu.VMEM((1, features), F32),
            pltpu.VMEM((qwidth, lat), BF16),
            pltpu.VMEM((2 * lat + 16, features), BF16),
            pltpu.VMEM((2, 3, rows + 2, width, chans), BF16),
            pltpu.VMEM((2, 9, chans, 3 * chans), BF16),
            pltpu.VMEM((3, features, qwidth), BF16),
            pltpu.VMEM((2, 2, rows, width, chans), BF16),
            pltpu.VMEM((2, 2, rows, width, chans), BF16),
            pltpu.VMEM((rows, width, chans), F32),
            pltpu.VMEM((2, rows * width // 2, lat), F32),
            pltpu.VMEM((n_aa, n_ba, tokens, lat), BF16),
            pltpu.VMEM((qwidth, 2 * lat), BF16),
            pltpu.VMEM((qwidth, 8), F32),
            pltpu.VMEM((2 * lat, qwidth), BF16),
            pltpu.VMEM((8, qwidth), F32),
            pltpu.VMEM((qwidth + 2 * lat, 2 * lat), BF16),
            pltpu.VMEM((qwidth, 8), F32),
            pltpu.VMEM((2 * lat, lat), BF16),
            pltpu.VMEM((lat + 8, lat + 8), F32),
            pltpu.VMEM((heads, SLOT, n_ba * tokens), BF16),
            pltpu.VMEM((heads // 2, total, SLOT), BF16),
            pltpu.VMEM((heads, STACK, total), BF16),
            pltpu.VMEM((qwidth, span), BF16),
            pltpu.VMEM((n_ba, lat, tokens), BF16),
            pltpu.VMEM((n_ba, lat, tokens), BF16),
            dma((10,)), dma((8,)),
            dma((2, 2, 2)), dma((2, 2, 2)), dma((2, 2)), dma((2, 2)),
            dma((n_aa, n_ba)), dma((n_aa,)), dma((n_aa, n_ba // 2)), dma((n_aa, n_ba // 2)),
            dma((n_ba,)), dma((n_ba,)),
        ],
        compiler_params=pltpu.CompilerParams(
            collective_id=0, has_side_effects=True, vmem_limit_bytes=VMEM_BYTES
        ),
        name="whole",
    )(
        feats, conv_one.reshape(3, 9, chans, chans), bias_one[None],
        conv_two.reshape(3, 9, chans, chans), bias_two[None],
        patch_weight, patch_bias[None], embed_weight, embed_bias[None], norm_gain[None],
        w_query, w_key, w_value, w_velocity,
    )


def solution(mesh):
    return jax.shard_map(
        functools.partial(on_device, mesh.shape["aa"], mesh.shape["ba"]),
        mesh=mesh,
        in_specs=(
            P("aa", "ba", None, None), P(), P(), P(), P(), P(), P(), P(), P(), P(),
            P(None, "ba"), P(None, "ba"), P(None, "ba"), P("ba", None),
        ),
        out_specs=P(("aa", "ba"), None),
        check_vma=False,
    )
```

```python
import functools
import math

import jax
import jax.numpy as jnp
from jax import lax
from jax.experimental import pallas as pl
from jax.experimental.pallas import tpu as pltpu
from jax.sharding import PartitionSpec as P

HEAD_DIM = 64
SLOT = 128
MESH = pl.DeviceIdType.MESH
LOOK = 1
GROUPED = 4
STACK = HEAD_DIM + 16
F32 = jnp.float32
BF16 = jnp.bfloat16
VMEM_BYTES = 67043328


def dot(left, right):
    return jnp.dot(left, right, preferred_element_type=F32)


def two_parts(value):
    high = value.astype(BF16)
    return high, (value - high.astype(F32)).astype(BF16)


def gelu(value):
    return 0.5 * value * (1.0 + lax.erf(value * (0.5**0.5)))


def whole_kernel(
    n_aa, n_ba, span, chunk,
    feats, conv_one, bias_one_in, conv_two, bias_two_in, patch_weight_in, patch_bias_in,
    embed_weight_in, embed_bias_in, norm_gain_in, w_query, w_key, w_value, w_velocity_in,
    out,
    bias_one, bias_two, patch_weight, patch_bias, embed_weight, embed_bias, norm_gain, w_velocity, gained,
    field, taps, w_joined, outgoing, incoming, acc, pair, gathered, turned_query, query_lift, split_key, key_offset, turned, lift,
    gram_split, gram, queries, keys, values, attended, shares, arrived,
    load_sem, small_sem, aa_side_send, aa_side_recv, ba_side_send, ba_side_recv,
    token_recv, aa_send, ba_send, core_send, share_send, share_recv,
):
    aa, ba = lax.axis_index("aa"), lax.axis_index("ba")
    _, rows, width, chans = feats.shape
    partner = ba + 1 - 2 * (ba % 2)
    half = n_ba // 2
    width_q = w_query.shape[1]
    heads = width_q // HEAD_DIM
    group_size = math.gcd(heads, GROUPED)
    tokens = rows * width // 4
    lat = patch_bias.shape[1]

    def load(source, target, at):
        return pltpu.make_async_copy(source, target, load_sem.at[at])

    loads = [
        load(feats.at[0], field.at[0, 1, pl.ds(1, rows)], 0),
        load(w_query, w_joined.at[0], 1),
        load(w_key, w_joined.at[1], 2),
        load(w_value, w_joined.at[2], 3),
    ]
    kernels = [
        [load(source.at[at], taps.at[which, :, :, pl.ds(column * chans, chans)], 4 + 3 * which + at)
         for at, column in enumerate((0, 2, 1))]
        for which, source in enumerate((conv_one, conv_two))
    ]
    small = [
        pltpu.make_async_copy(source, target, small_sem.at[at])
        for at, (source, target) in enumerate((
            (bias_one_in, bias_one), (embed_weight_in, embed_weight), (embed_bias_in, embed_bias),
            (norm_gain_in, norm_gain), (bias_two_in, bias_two), (patch_weight_in, patch_weight),
            (patch_bias_in, patch_bias), (w_velocity_in, w_velocity),
        ))
    ]
    loads[0].start()
    for at in (0, 2, 1):
        kernels[0][at].start()
    for one in small[:4]:
        one.start()
    for one in loads[1:]:
        one.start()
    for at in (0, 2, 1):
        kernels[1][at].start()
    for one in small[4:]:
        one.start()

    def aa_there(side):
        return aa > 0 if side == -1 else aa < n_aa - 1

    def ba_there(side):
        return ba > 0 if side == -1 else ba < n_ba - 1

    barrier = pltpu.get_barrier_semaphore()
    for step in range(1, n_aa):
        pl.semaphore_signal(
            barrier, inc=1, device_id=((aa + step) % n_aa, ba), device_id_type=MESH
        )
    for step in range(1, n_ba):
        pl.semaphore_signal(
            barrier, inc=1, device_id=(aa, (ba + step) % n_ba), device_id_type=MESH
        )

    edges, middle, both = 0, 1, 2
    parts = (slice(0, 2), slice(2, rows))

    def along_time(which, side, part):
        at = (which, (side + 1) // 2, part)
        here = (which, (side + 1) // 2, parts[part])
        return pltpu.make_async_remote_copy(
            src_ref=outgoing.at[here], dst_ref=incoming.at[here],
            send_sem=aa_side_send.at[at], recv_sem=aa_side_recv.at[at],
            device_id=(aa + side, ba), device_id_type=MESH,
        )

    def along_rows(which, side):
        source, target = (rows, 0) if side == 1 else (1, rows + 1)
        at = (which, (side + 1) // 2)
        return pltpu.make_async_remote_copy(
            src_ref=field.at[which, 1, source], dst_ref=field.at[which, 1, target],
            send_sem=ba_side_send.at[at], recv_sem=ba_side_recv.at[at],
            device_id=(aa, ba + side), device_id_type=MESH,
        )

    def send_rows(which):
        for side in (-1, 1):
            pl.when(ba_there(side))(along_rows(which, side).start)

    def take_rows(which):
        for side in (-1, 1):
            pl.when(ba_there(-side))(along_rows(which, side).wait_recv)
        shift(which, 0, 1)
        shift(which, rows + 1, 1)

    def take_time(which, part):
        for side in (-1, 1):
            pl.when(aa_there(-side))(along_time(which, side, part).wait_recv)

    def sent(which):
        for side in (-1, 1):
            pl.when(ba_there(side))(along_rows(which, side).wait_send)
            for part in (edges, middle):
                pl.when(aa_there(side))(along_time(which, side, part).wait_send)

    def blank():
        line = jnp.zeros((width, chans), BF16)
        for which in range(2):
            for side, row in ((-1, 0), (1, rows + 1)):
                @pl.when(jnp.logical_not(ba_there(side)))
                def _():
                    field[which, 1, row] = line

                @pl.when(jnp.logical_not(aa_there(side)))
                def _():
                    for at in range(rows):
                        incoming[which, (1 - side) // 2, at] = line

    def shift(which, row, count):
        here = pl.ds(row, count)
        held = field[which, 1, here].reshape(count * width, chans).astype(F32)
        place = lax.broadcasted_iota(jnp.int32, held.shape, 0) % width
        before = jnp.where(place == 0, 0.0, pltpu.roll(held, 1, 0))
        after = jnp.where(place == width - 1, 0.0, pltpu.roll(held, count * width - 1, 0))
        field[which, 0, here] = before.astype(BF16).reshape(count, width, chans)
        field[which, 2, here] = after.astype(BF16).reshape(count, width, chans)

    def stack(which, part):
        def window(shift_r, shift_w):
            if part == middle:
                held = field[which, shift_w, pl.ds(1 + shift_r, rows - 2)]
                return held.reshape((rows - 2) * width, chans)
            if part == both:
                return field[which, shift_w, pl.ds(shift_r, rows)].reshape(rows * width, chans)
            return jnp.concatenate(
                [field[which, shift_w, shift_r], field[which, shift_w, rows - 1 + shift_r]], axis=0
            )

        return jnp.concatenate(
            [window(shift_r, shift_w) for shift_r in range(3) for shift_w in range(3)], axis=1
        )

    def send_time(which, part):
        made = dot(
            stack(which, part), taps[which, :, :, : 2 * chans].reshape(9 * chans, 2 * chans)
        ).astype(BF16)
        for side, column in ((-1, chans), (1, 0)):
            outgoing[which, (side + 1) // 2, parts[part]] = made[
                :, column : column + chans
            ].reshape(-1, width, chans)
            pl.when(aa_there(side))(along_time(which, side, part).start)

    def keep(which):
        acc[...] = dot(
            stack(which, both), taps[which, :, :, 2 * chans :].reshape(9 * chans, chans)
        ).reshape(rows, width, chans)

    def activate(which, part, bias):
        here = parts[part]
        kept = acc[1 : rows - 1] if part == middle else jnp.concatenate(
            [acc[:1], acc[rows - 1 :]], axis=0
        )
        total = kept + incoming[which, 0, here].astype(F32)
        total += incoming[which, 1, here].astype(F32)
        return gelu(total.reshape(-1, chans) + bias)

    blank()
    loads[0].wait()
    shift(0, 1, rows)
    pl.semaphore_wait(barrier, n_aa - 1 + n_ba - 1)
    send_rows(0)
    kernels[0][0].wait()
    kernels[0][2].wait()
    send_time(0, middle)
    take_rows(0)
    send_time(0, edges)

    def merge_gram():
        for one in small[:4]:
            one.wait()
        embed = embed_weight[...].astype(F32)
        centred = jnp.concatenate(
            [
                embed - embed.mean(-1, keepdims=True),
                jnp.broadcast_to(
                    embed_bias[...] - embed_bias[...].mean(-1, keepdims=True),
                    (8, embed.shape[1]),
                ),
            ],
            axis=0,
        )
        gram[...] = lax.dot_general(
            centred, centred, (((1,), (1,)), ((), ())),
            precision=lax.Precision.HIGHEST, preferred_element_type=F32,
        ) * (1.0 / embed.shape[1])
        high, low = two_parts(gram[:lat, :lat])
        gram_split[:lat] = high
        gram_split[lat:] = low
        turned[width_q : width_q + lat, :lat] = high
        turned[width_q : width_q + lat, lat:] = low
        across = lax.broadcasted_iota(jnp.int32, (lat, 2 * lat), 1)
        down = lax.broadcasted_iota(jnp.int32, (lat, 2 * lat), 0)
        turned[width_q + lat :] = (across == down).astype(BF16)
        gained[...] = jnp.concatenate(two_parts(centred * norm_gain[...]), axis=0)

    def merge(which):
        loads[1 + which].wait()
        product = dot(gained[...], w_joined[which])
        product = product[: lat + 8] + product[lat + 8 :]
        if which == 0:
            product = product * (HEAD_DIM**-0.5 * math.log2(math.e))
            high, low = two_parts(product[:lat].T)
            turned_query[:, :lat] = high
            turned_query[:, lat:] = low
            query_lift[...] = product[lat:].T
        elif which == 1:
            high, low = two_parts(product[:lat])
            split_key[:lat] = high
            split_key[lat:] = low
            key_offset[...] = product[lat:]
        else:
            high, low = two_parts(product[:lat].T)
            turned[:width_q, :lat] = high
            turned[:width_q, lat:] = low
            lift[...] = product[lat:].T

    kernels[0][1].wait()
    keep(0)
    merge_gram()
    merge(2)
    take_time(0, middle)
    first = activate(0, middle, bias_one[...]).astype(BF16)
    field[1, 1, 2:rows] = first.reshape(-1, width, chans)
    shift(1, 2, rows - 2)
    take_time(0, edges)
    first = activate(0, edges, bias_one[...]).astype(BF16)
    field[1, 1, 1] = first[:width]
    field[1, 1, rows] = first[width:]
    send_rows(1)
    shift(1, 1, 1)
    shift(1, rows, 1)
    for at in (0, 2, 1):
        kernels[1][at].wait()
    send_time(1, middle)
    merge(1)
    take_rows(1)
    send_time(1, edges)
    keep(1)
    merge(0)
    for one in small[4:]:
        one.wait()

    def finish(part):
        here = field[1, 1, 2:rows] if part == middle else jnp.concatenate(
            [field[1, 1, 1], field[1, 1, rows]], axis=0
        )
        own = here.reshape(-1, chans).astype(F32)
        return (own + activate(1, part, bias_two[...])).astype(BF16)

    take_time(1, middle)
    inner = finish(middle)
    take_time(1, edges)
    outer = finish(edges)
    lines = [outer[:width]]
    lines += [inner[at * width : (at + 1) * width] for at in range(rows - 2)]
    lines += [outer[width:]]

    stacked = jnp.concatenate(
        [jnp.concatenate(lines[2 * block : 2 * block + 2], axis=1) for block in range(rows // 2)],
        axis=0,
    )
    square = jnp.concatenate(
        [jnp.concatenate([patch_weight[row, col] for col in range(2)], axis=1) for row in range(2)],
        axis=0,
    )
    both_columns = dot(stacked, square)
    for col in range(2):
        pair[col] = both_columns[:, col * lat : (col + 1) * lat]
    patches = (
        pair[0, pl.ds(0, tokens, stride=2), :] + pair[1, pl.ds(1, tokens, stride=2), :]
        + patch_bias[...]
    ).astype(BF16)
    gathered[aa, ba] = patches

    for head in range(heads):
        slot = slice((1 - head % 2) * HEAD_DIM, (2 - head % 2) * HEAD_DIM)
        queries[head, slot] = jnp.zeros((HEAD_DIM, queries.shape[2]), BF16)
    values[:, HEAD_DIM:] = jnp.ones((heads, values.shape[1] - HEAD_DIM, values.shape[2]), BF16)

    flanked = jnp.minimum(aa, n_aa - 1 - aa)
    toward = jnp.where(aa < n_aa - 1 - aa, 1, -1)

    def frame_of(step):
        near = (1 - 2 * ((step + 1) % 2)) * ((step + 1) // 2)
        return aa + jnp.where(step <= 2 * flanked, near, toward * (step - flanked))

    def piece(frame, block, send_sem, to_aa, to_ba):
        here = gathered.at[frame, block]
        return pltpu.make_async_remote_copy(
            src_ref=here, dst_ref=here, send_sem=send_sem, recv_sem=token_recv.at[frame, block],
            device_id=(to_aa, to_ba), device_id_type=MESH,
        )

    def along_aa(step):
        return piece(aa, ba, aa_send.at[step], frame_of(step), ba)

    def along_ba(step, hop):
        return piece(frame_of(step), ba, ba_send.at[step, hop], aa, (ba + 2 * hop) % n_ba)

    def to_partner(step, hop):
        block = (ba + n_ba - 2 * hop) % n_ba
        return piece(frame_of(step), block, core_send.at[step, hop], aa, partner)

    def landed(frame, block):
        piece(frame, block, aa_send.at[0], aa, partner).wait_recv()

    slope = 2.0 * gram[lat : lat + 1, :lat]
    slope_down = 2.0 * gram[:lat, lat : lat + 1]
    floor = gram[lat : lat + 1, lat : lat + 1]

    def take_pairs(step, hops, with_queries):
        frame = frame_of(step)
        blocks = [((ba + n_ba - 2 * hop) % n_ba) // 2 for hop in hops]
        size = 2 * tokens
        latents = jnp.concatenate(
            [gathered[frame, pl.ds(2 * block, 2)].reshape(size, lat) for block in blocks], axis=0
        )
        twice = jnp.concatenate([latents, latents], axis=1)
        bent = dot(twice, gram_split[...]) + slope
        power = (bent * latents.astype(F32)).sum(-1, keepdims=True) + floor
        scale = lax.rsqrt(jnp.maximum(power, 0.0) + 1e-05)
        projected = ((dot(twice, split_key[...]) + key_offset[:1]) * scale).astype(BF16)
        down = lax.dot_general(
            turned[...], twice, (((1,), (1,)), ((), ())), preferred_element_type=F32
        )
        bent = (down[width_q : width_q + lat] + slope_down) * down[width_q + lat :]
        power = bent.sum(0, keepdims=True) + floor
        scale_down = lax.rsqrt(jnp.maximum(power, 0.0) + 1e-05)
        flipped = ((down[:width_q] + lift[:, :1]) * scale_down).astype(BF16)
        for index, block in enumerate(blocks):
            own = slice(index * size, (index + 1) * size)
            at = pl.ds(pl.multiple_of((frame * half + block) * size, size), size)
            for couple in range(heads // 2):
                keys[couple, at] = projected[own, couple * SLOT : (couple + 1) * SLOT]
            for head in range(heads):
                values[head, :HEAD_DIM, at] = flipped[head * HEAD_DIM : (head + 1) * HEAD_DIM, own]
        if with_queries:
            down = lax.dot_general(
                turned_query[...], twice, (((1,), (1,)), ((), ())), preferred_element_type=F32
            )
            asked = ((down + query_lift[:, :1]) * scale_down).astype(BF16)
            for index, block in enumerate(blocks):
                own = slice(index * size, (index + 1) * size)
                there = pl.ds(pl.multiple_of(block * size, size), size)
                for head in range(heads):
                    slot = slice(head % 2 * HEAD_DIM, (head % 2 + 1) * HEAD_DIM)
                    queries[head, slot, there] = asked[head * HEAD_DIM : (head + 1) * HEAD_DIM, own]

    def pass_on(step):
        for hop in range(1, half):
            along_ba(step, hop).start()
        to_partner(step, 0).start()

    def advance(step):
        landed(frame_of(step), ba)
        pass_on(step)

    def hand_over(step):
        @pl.loop(1, half)
        def _(hop):
            landed(frame_of(step), (ba + n_ba - 2 * hop) % n_ba)
            to_partner(step, hop).start()

    def take(step, hop, with_queries):
        landed(frame_of(step), (partner + n_ba - 2 * hop) % n_ba)
        take_pairs(step, [hop], with_queries)

    def take_all(pairs, with_queries):
        for step, hop in pairs:
            landed(frame_of(step), (partner + n_ba - 2 * hop) % n_ba)
        for step, hop in pairs:
            take_pairs(step, [hop], with_queries)

    def take_rest(step, also, with_queries):
        batch = max(each for each in (1, 2, 3) if (half - 1) % each == 0)

        @pl.loop(0, (half - 1) // batch - 1)
        def _(index):
            take_all([(step, 1 + index * batch + each) for each in range(batch)], with_queries)

        take_all([(step, half - 1 - each) for each in range(batch)] + also, with_queries)

    for step in range(1, n_aa):
        along_aa(step).start()
    pass_on(0)
    sent(0)
    sent(1)
    take(0, 0, True)
    advance(1)
    hand_over(0)

    @pl.loop(1, half)
    def _(hop):
        take(0, hop, True)
        pl.when(hop + 1 < n_aa)(lambda: advance(hop + 1))

    for step in range(half + 1, n_aa):
        advance(step)
    for step in range(1, n_aa, 3):
        take_all([(each, 0) for each in range(step, min(step + 3, n_aa))], False)
    hand_over(1)

    @pl.loop(2, n_aa)
    def _(step):
        hand_over(step)
        take_rest(step - 1, [], False)

    take_rest(n_aa - 1, [], False)

    for step in range(1, n_aa):
        along_aa(step).wait_send()

    @pl.loop(0, n_aa)
    def _(step):
        to_partner(step, 0).wait_send()

        @pl.loop(1, half)
        def _(hop):
            along_ba(step, hop).wait_send()
            to_partner(step, hop).wait_send()

    def share(dest):
        offset = (dest + n_ba - ba) % n_ba
        return pltpu.make_async_remote_copy(
            src_ref=shares.at[dest], dst_ref=arrived.at[ba],
            send_sem=share_send.at[offset], recv_sem=share_recv.at[offset],
            device_id=(aa, dest), device_id_type=MESH,
        )

    total = keys.shape[1]
    big = math.gcd(total, 4096)

    def attend(at):
        per_span = span // tokens
        where = pl.ds(pl.multiple_of(at * span, span), span)

        def sweep(group, asked, base, state):
            order = [(each, part) for each in range(len(asked)) for part in range(big // chunk)]

            def held(part):
                return pl.ds(pl.multiple_of(base + part * chunk, chunk), chunk)

            def score(each, part):
                return dot(keys[(group + each) // 2, held(part)], asked[each])

            def gather(each, part, shrink, probs):
                best, accum = state[each]
                added = dot(values[group + each, :, held(part)], probs)
                return added if shrink is None else accum * shrink + added

            ahead = [score(*one) for one in order[:LOOK]]
            late = None
            for index, (each, part) in enumerate(order):
                if index + LOOK < len(order):
                    ahead.append(score(*order[index + LOOK]))
                scores, ahead[index] = ahead[index], None
                best, accum = state[each]
                peak = scores.max(0, keepdims=True)
                shrink = None
                if best is not None:
                    peak = jnp.maximum(best, peak)
                    shrink = jnp.exp2(best - peak)
                probs = jnp.exp2(scores - peak).astype(BF16)
                if late is not None:
                    state[late[0]] = (state[late[0]][0], gather(*late))
                state[each] = (peak, state[each][1])
                late = (each, part, shrink, probs)
            state[late[0]] = (state[late[0]][0], gather(*late))
            return state

        @pl.loop(0, heads // group_size)
        def _(index):
            group = index * group_size
            asked = [queries[group + each, :, where] for each in range(group_size)]
            if total == big:
                state = sweep(group, asked, 0, [(None, None)] * group_size)
            else:
                empty = (jnp.full((1, span), -jnp.inf, F32), jnp.zeros((values.shape[1], span), F32))

                def one_big(index, state):
                    return tuple(sweep(group, asked, index * big, list(state)))

                state = lax.fori_loop(0, total // big, one_big, (empty,) * group_size)
            for each in range(group_size):
                accum = state[each][1]
                rows = pl.ds(pl.multiple_of((group + each) * HEAD_DIM, HEAD_DIM), HEAD_DIM)
                attended[rows] = (accum[:HEAD_DIM] / accum[HEAD_DIM : HEAD_DIM + 1]).astype(BF16)

        velocity = lax.dot_general(
            w_velocity[...], attended[...], (((0,), (0,)), ((), ())), preferred_element_type=F32
        )
        for part in range(per_span):
            dest = at * per_span + part
            shares[dest] = velocity[:, part * tokens : (part + 1) * tokens].astype(BF16)

            @pl.when(dest != ba)
            def _():
                share(dest).start()

    spans = n_ba * tokens // span

    @pl.loop(1, spans + 1)
    def _(step):
        attend((ba * tokens // span + step) % spans)

    summed = shares[ba].astype(F32)
    for offset in range(1, n_ba):
        share((ba + offset) % n_ba).wait_recv()
        summed += arrived[(ba + n_ba - offset) % n_ba].astype(F32)
    out[...] = summed.T
    for offset in range(1, n_ba):
        share((ba + offset) % n_ba).wait_send()


def on_device(
    n_aa, n_ba,
    feats, conv_one, bias_one, conv_two, bias_two, patch_weight, patch_bias,
    embed_weight, embed_bias, norm_gain, w_query, w_key, w_value, w_velocity,
):
    _, rows, width, chans = feats.shape
    lat = patch_bias.shape[0]
    features, qwidth = w_query.shape
    heads = qwidth // HEAD_DIM
    tokens = rows * width // 4
    total = n_ba * n_aa * tokens
    span = max(tokens, min(512, n_ba * tokens))
    chunk = math.gcd(total, 256)
    vmem = pl.BlockSpec(memory_space=pltpu.VMEM)
    anywhere = pl.BlockSpec(memory_space=pl.ANY)
    dma = pltpu.SemaphoreType.DMA
    return pl.pallas_call(
        functools.partial(whole_kernel, n_aa, n_ba, span, chunk),
        out_shape=jax.ShapeDtypeStruct((tokens, lat), F32),
        in_specs=[anywhere] * 14,
        out_specs=vmem,
        scratch_shapes=[
            pltpu.VMEM((1, chans), F32),
            pltpu.VMEM((1, chans), F32),
            pltpu.VMEM((2, 2, chans, lat), BF16),
            pltpu.VMEM((1, lat), F32),
            pltpu.VMEM((lat, features), BF16),
            pltpu.VMEM((1, features), F32),
            pltpu.VMEM((1, features), F32),
            pltpu.VMEM((qwidth, lat), BF16),
            pltpu.VMEM((2 * lat + 16, features), BF16),
            pltpu.VMEM((2, 3, rows + 2, width, chans), BF16),
            pltpu.VMEM((2, 9, chans, 3 * chans), BF16),
            pltpu.VMEM((3, features, qwidth), BF16),
            pltpu.VMEM((2, 2, rows, width, chans), BF16),
            pltpu.VMEM((2, 2, rows, width, chans), BF16),
            pltpu.VMEM((rows, width, chans), F32),
            pltpu.VMEM((2, rows * width // 2, lat), F32),
            pltpu.VMEM((n_aa, n_ba, tokens, lat), BF16),
            pltpu.VMEM((qwidth, 2 * lat), BF16),
            pltpu.VMEM((qwidth, 8), F32),
            pltpu.VMEM((2 * lat, qwidth), BF16),
            pltpu.VMEM((8, qwidth), F32),
            pltpu.VMEM((qwidth + 2 * lat, 2 * lat), BF16),
            pltpu.VMEM((qwidth, 8), F32),
            pltpu.VMEM((2 * lat, lat), BF16),
            pltpu.VMEM((lat + 8, lat + 8), F32),
            pltpu.VMEM((heads, SLOT, n_ba * tokens), BF16),
            pltpu.VMEM((heads // 2, total, SLOT), BF16),
            pltpu.VMEM((heads, STACK, total), BF16),
            pltpu.VMEM((qwidth, span), BF16),
            pltpu.VMEM((n_ba, lat, tokens), BF16),
            pltpu.VMEM((n_ba, lat, tokens), BF16),
            dma((10,)), dma((8,)),
            dma((2, 2, 2)), dma((2, 2, 2)), dma((2, 2)), dma((2, 2)),
            dma((n_aa, n_ba)), dma((n_aa,)), dma((n_aa, n_ba // 2)), dma((n_aa, n_ba // 2)),
            dma((n_ba,)), dma((n_ba,)),
        ],
        compiler_params=pltpu.CompilerParams(
            collective_id=0, has_side_effects=True, vmem_limit_bytes=VMEM_BYTES
        ),
        name="whole",
    )(
        feats, conv_one.reshape(3, 9, chans, chans), bias_one[None],
        conv_two.reshape(3, 9, chans, chans), bias_two[None],
        patch_weight, patch_bias[None], embed_weight, embed_bias[None], norm_gain[None],
        w_query, w_key, w_value, w_velocity,
    )


def solution(mesh):
    return jax.shard_map(
        functools.partial(on_device, mesh.shape["aa"], mesh.shape["ba"]),
        mesh=mesh,
        in_specs=(
            P("aa", "ba", None, None), P(), P(), P(), P(), P(), P(), P(), P(), P(),
            P(None, "ba"), P(None, "ba"), P(None, "ba"), P("ba", None),
        ),
        out_specs=P(("aa", "ba"), None),
        check_vma=False,
    )
```
